32 devices in a mesh: scan: 8 (over z, y), beam: 4 (over x, core).
Axes of the slice: x: 2, y: 2, z: 4, core: 2. Of those that a mesh axis runs over, the one named last changes fastest.
Arguments:
- smatrix: bfloat16 [2, 1024, 512, 128], P(None, 'beam', 'scan'), may hold values from -6 to 6
- beam_freq: int32 [2, 1024], P(None, 'beam'), may hold values from -32 to 31
- beam_amp: float32 [2, 1024], P(None, 'beam'), may hold values from -0.1875 to 0.1875
- row_offset: int32 [512], P('scan'), may hold values from 0 to 63
- col_offset: int32 [512], P('scan'), may hold values from 0 to 127
- counts: int32 [8], P('scan'), may hold values from 16 to 64, as said below
- amplitude: float32 [512, 128, 128], P('scan'), may hold values from 0.25 to 2
Outputs:
- grad_smatrix: bfloat16 [2, 1024, 512, 128], P(None, 'beam', 'scan')
The draws below stay inside these ranges and needn't reach their ends.
Inputs may be any that keep to these rules, and one draw needn't show every extreme that they name: `counts`: slots of a tile at or past its count are unused; some tile holds exactly 64 live positions.
All inputs are finite; a program needn't handle non-finite values.
Results may differ from the reference program's by a relative error of at most 0.0063.
Values may be sent and summed in bfloat16 or wider, within the bound.
A program may use at most 192 MiB of HBM per device.

```python
import math
import jax
import jax.numpy as jnp
from jax import lax

WIN = 128
BEAMS = 1024
POS_DEV = 64
TY = 64
NY = 512
POSITIONS = 512
N_SCAN = 8


def draw_counts(key, part):
    first_key = jax.random.fold_in(key, 11)
    second_key = jax.random.fold_in(key, 12)
    values = jax.random.randint(first_key, (N_SCAN,), max(1, POS_DEV // 4), POS_DEV + 1)
    chosen = jax.random.randint(second_key, (), 0, N_SCAN)
    return jnp.where(jnp.arange(N_SCAN) == chosen, POS_DEV, values).astype(jnp.int32)


def set_ends(values, own_key, low, largest):
    longest = values.shape.index(max(values.shape))
    spots = []
    for shift in (0, 1):
        where = [jax.random.randint(jax.random.fold_in(own_key, axis), (), 0, length) for axis, length in enumerate(values.shape)]
        where[longest] = (where[longest] + shift) % values.shape[longest]
        spots.append(tuple(where))
    return values.at[spots[0]].set(low).at[spots[1]].set(largest)


def steps_of(stream_key, dims, pieces, smallest, high):
    def one(dim, parts):
        draws = jax.random.uniform(jax.random.fold_in(jax.random.fold_in(stream_key, 6), dim), (parts,), jnp.float32, smallest / len(pieces), high / len(pieces))
        return jnp.repeat(jnp.exp(draws), dims[dim] // parts).reshape((-1,) + (1,) * (len(dims) - dim - 1))

    loudness = one(*pieces[0])
    for cut in pieces[1:]:
        loudness = loudness * one(*cut)
    return loudness


def scatter_about(rng, dims, width, most, cuts=(), kind=jnp.bfloat16):
    result = width * jax.random.normal(rng, dims, jnp.float32)
    if cuts:
        result = result * steps_of(rng, dims, cuts, -0.22, 0.18)
    return jnp.clip(result, -most, most).astype(kind)


def setup_inputs(seed: int = 0) -> dict:
    key_list = jax.random.split(jax.random.key(seed), 8)
    return {
        "smatrix": scatter_about(key_list[0], (2, BEAMS, NY, WIN), 1.0, 6.0, ((1, 4), (2, 8))),
        "beam_freq": set_ends(jax.random.randint(key_list[1], (2, BEAMS), 0 - WIN // 4, WIN // 4), jax.random.fold_in(key_list[1], 1), 0 - WIN // 4, (WIN // 4) - 1).astype(jnp.int32),
        "beam_amp": scatter_about(key_list[2], (2, BEAMS), BEAMS ** -0.5, 0.1875, ((1, 4),), jnp.float32),
        "row_offset": set_ends(jax.random.randint(key_list[3], (POSITIONS,), 0, TY), jax.random.fold_in(key_list[3], 1), 0, TY - 1).astype(jnp.int32),
        "col_offset": set_ends(jax.random.randint(key_list[4], (POSITIONS,), 0, WIN), jax.random.fold_in(key_list[4], 1), 0, WIN - 1).astype(jnp.int32),
        "counts": draw_counts(jax.random.fold_in(key_list[7], 71), 0),
        "amplitude": jnp.clip(0.25 + 1.75 * jax.random.uniform(key_list[6], (POSITIONS, WIN, WIN), jnp.float32) ** steps_of(key_list[6], (POSITIONS, WIN, WIN), ((0, 8),), -0.2, 0.2), 0.25, 2.0),
    }


TWO_PI = 6.283185307179586
ETA = 0.1

def coefficients(tile_rows, tile_cols, tile_ids, beam_freq, beam_amp, strip_rows, field_rows, window):
    global_rows = tile_ids * strip_rows + tile_rows
    along_rows = beam_freq[0][None, :] * global_rows[:, None] % field_rows
    along_cols = beam_freq[1][None, :] * tile_cols[:, None] % window
    phase_turns = along_rows.astype(jnp.float32) / field_rows + along_cols.astype(jnp.float32) / window
    phase_angle = -TWO_PI * phase_turns
    cos_part = jnp.cos(phase_angle)
    sin_part = jnp.sin(phase_angle)
    coef_re = beam_amp[0][None, :] * cos_part - beam_amp[1][None, :] * sin_part
    coef_im = beam_amp[0][None, :] * sin_part + beam_amp[1][None, :] * cos_part
    return (coef_re.astype(jnp.bfloat16), coef_im.astype(jnp.bfloat16))

def forward_matrix(coef_re, coef_im):
    real_rows = jnp.concatenate([coef_re, -coef_im], axis=1)
    imag_rows = jnp.concatenate([coef_im, coef_re], axis=1)
    return jnp.concatenate([real_rows, imag_rows], axis=0)

def backward_matrix(coef_re, coef_im):
    real_rows = jnp.concatenate([coef_re.T, coef_im.T], axis=1)
    imag_rows = jnp.concatenate([-coef_im.T, coef_re.T], axis=1)
    return jnp.concatenate([real_rows, imag_rows], axis=0)

def dft_tables(window):
    counter = jnp.arange(window, dtype=jnp.int32)
    product = counter[:, None] * counter[None, :] % window
    turn_angle = product.astype(jnp.float32) * (TWO_PI / window)
    norm_scale = 1.0 / math.sqrt(window)
    return (jnp.cos(turn_angle) * norm_scale, -jnp.sin(turn_angle) * norm_scale)

def transform(real_in, imag_in, table_re, table_im):
    highest = lax.Precision.HIGHEST
    left_re = jnp.einsum('jk,qkl->qjl', table_re, real_in, precision=highest) - jnp.einsum('jk,qkl->qjl', table_im, imag_in, precision=highest)
    left_im = jnp.einsum('jk,qkl->qjl', table_re, imag_in, precision=highest) + jnp.einsum('jk,qkl->qjl', table_im, real_in, precision=highest)
    out_re = jnp.einsum('qjk,kl->qjl', left_re, table_re, precision=highest) - jnp.einsum('qjk,kl->qjl', left_im, table_im, precision=highest)
    out_im = jnp.einsum('qjk,kl->qjl', left_re, table_im, precision=highest) + jnp.einsum('qjk,kl->qjl', left_im, table_re, precision=highest)
    return (out_re, out_im)

def far_field_gradient(wave_re, wave_im, measured, live_rows, tables):
    table_re, table_im = tables
    far_re, far_im = transform(wave_re, wave_im, table_re, table_im)
    modulus = jnp.sqrt(far_re * far_re + far_im * far_im + ETA)
    keep_share = 1.0 - measured / modulus
    back_re, back_im = transform(far_re * keep_share, far_im * keep_share, table_re, -table_im)
    live_mask = live_rows[:, None, None]
    return jnp.stack([back_re * live_mask, back_im * live_mask], axis=0).astype(jnp.bfloat16)

def selection(tile_rows, window, total_rows):
    field_index = jnp.arange(total_rows, dtype=jnp.int32)
    window_index = jnp.arange(window, dtype=jnp.int32)
    target = tile_rows[:, None, None] + window_index[None, None, :]
    return (field_index[None, :, None] == target).astype(jnp.float32)

def take_window(strip_waves, tile_rows, window):
    picker = selection(tile_rows, window, strip_waves.shape[2])
    return jnp.einsum('pyj,cpyx->cpjx', picker, strip_waves.astype(jnp.float32), precision=lax.Precision.HIGHEST)

def place_rows(wave_grads, tile_rows, total_rows):
    picker = selection(tile_rows, wave_grads.shape[2], total_rows)
    placed = jnp.einsum('pyj,cpjx->cpyx', picker, wave_grads.astype(jnp.float32))
    return placed.astype(jnp.bfloat16)

def reference(smatrix, beam_freq, beam_amp, row_offset, col_offset, counts, amplitude):
    tables = dft_tables(WIN)
    field_rows = TY * N_SCAN

    def tile_coefficients(tile_id):
        tile_rows = lax.dynamic_slice_in_dim(row_offset, tile_id * POS_DEV, POS_DEV)
        tile_cols = lax.dynamic_slice_in_dim(col_offset, tile_id * POS_DEV, POS_DEV)
        tile_ids = jnp.full((POS_DEV,), tile_id, jnp.int32)
        return (tile_rows, coefficients(tile_rows, tile_cols, tile_ids, beam_freq, beam_amp, TY, field_rows, WIN))

    def strip_of(strip_index):
        return lax.dynamic_slice_in_dim(smatrix, (strip_index % N_SCAN * TY).astype(jnp.int32), TY, axis=2)

    def forward_tile(tile_id):
        tile_rows, (coef_re, coef_im) = tile_coefficients(tile_id)
        extended = jnp.concatenate([strip_of(tile_id + distance) for distance in range(3)], axis=2).reshape(2 * BEAMS, 3 * TY * WIN)
        strip_waves = jnp.dot(forward_matrix(coef_re, coef_im), extended, preferred_element_type=jnp.float32).reshape(2, POS_DEV, 3 * TY, WIN)
        windows = take_window(strip_waves, tile_rows, WIN)
        live_rows = (jnp.arange(POS_DEV, dtype=jnp.int32) < lax.dynamic_index_in_dim(counts, tile_id, keepdims=False)).astype(jnp.float32)
        measured = lax.dynamic_slice_in_dim(amplitude, tile_id * POS_DEV, POS_DEV)
        return far_field_gradient(windows[0], windows[1], measured, live_rows, tables)
    tile_list = jnp.arange(N_SCAN, dtype=jnp.int32)
    all_grads = lax.map(forward_tile, tile_list)

    def strip_gradient(strip_id):
        grad_parts = []
        re_parts = []
        im_parts = []
        for distance in range(3):
            tile_id = ((strip_id - distance) % N_SCAN).astype(jnp.int32)
            tile_rows, (coef_re, coef_im) = tile_coefficients(tile_id)
            wave_grads = lax.dynamic_index_in_dim(all_grads, tile_id, keepdims=False)
            placed = place_rows(wave_grads, tile_rows, 3 * TY)
            grad_parts.append(placed[:, :, distance * TY:(distance + 1) * TY])
            re_parts.append(coef_re)
            im_parts.append(coef_im)
        gathered = jnp.stack(grad_parts, axis=1).reshape(6 * POS_DEV, TY * WIN)
        matrix = backward_matrix(jnp.concatenate(re_parts, axis=0), jnp.concatenate(im_parts, axis=0))
        return jnp.dot(matrix, gathered, preferred_element_type=jnp.float32).astype(jnp.bfloat16).reshape(2, BEAMS, TY, WIN)
    strips = lax.map(strip_gradient, tile_list)
    return jnp.transpose(strips, (1, 2, 0, 3, 4)).reshape(2, BEAMS, N_SCAN * TY, WIN)
```

```python
import functools

import jax
import jax.numpy as jnp
import numpy as np
from jax import lax
from jax.experimental import pallas as pl
from jax.experimental.pallas import tpu as pltpu
from jax.sharding import PartitionSpec as P

TWO_PI = 6.283185307179586
ETA = 0.1
GROUPS = 2
F32 = jnp.float32
BF16 = jnp.bfloat16
MESH = pl.DeviceIdType.MESH


def passed_along(value, axis, by):
    devices = lax.axis_size(axis)
    return lax.ppermute(value, axis, [(i, (i + by) % devices) for i in range(devices)])


def coefficients(
    global_rows, tile_cols, beam_freq, beam_amp, field_rows, window
):
    along_rows = beam_freq[0][None, :] * global_rows[:, None] % field_rows
    along_cols = beam_freq[1][None, :] * tile_cols[:, None] % window
    phase_turns = along_rows.astype(F32) / field_rows + along_cols.astype(F32) / window
    phase_angle = -TWO_PI * phase_turns
    cos_part = jnp.cos(phase_angle)
    sin_part = jnp.sin(phase_angle)
    coef_re = beam_amp[0][None, :] * cos_part - beam_amp[1][None, :] * sin_part
    coef_im = beam_amp[0][None, :] * sin_part + beam_amp[1][None, :] * cos_part
    return (coef_re.astype(BF16), coef_im.astype(BF16))


def split_two(value):
    high = value.astype(BF16)
    return high, (value - high.astype(F32)).astype(BF16)


def forward_kernel(shares, scan_size, bounds_ref, matrix_ref, strip_ref, near_ref, far_ref,
                   strips, wide, kept, core_out, core_in, link_out, link_in, scan_out, scan_in,
                   load_sem, core_send, core_recv, link_send, link_recv, scan_send, scan_recv):
    chunks, pairs, _, block_rows, group, window = kept.shape
    beams = strip_ref.shape[1]
    depth = 2 * beams
    me = lax.axis_index("beam")
    tile = lax.axis_index("scan")
    core_mate = {"beam": me + 1 - 2 * lax.rem(me, 2)}
    link_mate = {"beam": lax.rem(me + shares // 2, shares)}
    owners = [{"scan": lax.rem(tile + scan_size - d, scan_size)} for d in (1, 2)]
    givers = [{"scan": lax.rem(tile + d, scan_size)} for d in (1, 2)]

    def load(chunk):
        return pltpu.make_async_copy(
            strip_ref.at[:, :, pl.ds(chunk * block_rows, block_rows), :],
            strips.at[chunk % 2],
            load_sem.at[chunk % 2],
        )

    def to_core(chunk):
        return pltpu.make_async_remote_copy(
            core_out.at[chunk], core_in.at[chunk], core_send.at[chunk], core_recv.at[chunk],
            device_id=core_mate, device_id_type=MESH,
        )

    def to_link(chunk):
        return pltpu.make_async_remote_copy(
            link_out.at[chunk], link_in.at[chunk], link_send.at[chunk], link_recv.at[chunk],
            device_id=link_mate, device_id_type=MESH,
        )

    def to_scan(chunk, which):
        return pltpu.make_async_remote_copy(
            scan_out.at[chunk, which], scan_in.at[chunk, which],
            scan_send.at[chunk, which], scan_recv.at[chunk, which],
            device_id=owners[which], device_id_type=MESH,
        )

    load(0).start()
    load(1).start()
    barrier = pltpu.get_barrier_semaphore()
    peers = [core_mate, link_mate] + owners + givers
    for peer in peers:
        pl.semaphore_signal(barrier, inc=1, device_id=peer, device_id_type=MESH)
    pl.semaphore_wait(barrier, len(peers))

    def compute(chunk):
        load(chunk).wait()
        wide[...] = strips[chunk % 2].astype(F32).reshape(depth * block_rows, window)
        if chunk + 2 < chunks:
            load(chunk + 2).start()

        def pair_of_rows(step, carry):
            row = step * 2
            rhs = jnp.concatenate(
                [wide[pl.ds(row + k, depth, stride=block_rows), :] for k in range(2)], axis=1
            ).astype(BF16)
            sums = jnp.dot(matrix_ref[...], rhs, preferred_element_type=F32)
            for k in range(2):
                here = chunk * block_rows + row + k
                inside = (bounds_ref[0] <= here) & (here < bounds_ref[1])
                part = jnp.where(inside, sums[:, k * window : (k + 1) * window], 0.0)
                for d in range(3):
                    for share in range(shares):
                        at = (d * shares + share) * group
                        piece = part[at : at + group]
                        if share < pairs:
                            kept[chunk, share, d, row + k] = piece
                        else:
                            core_out[chunk, share - pairs, d, row + k] = piece.astype(BF16)
            return carry

        lax.fori_loop(0, block_rows // 2, pair_of_rows, 0)
        to_core(chunk).start()

    def over_link(chunk):
        to_core(chunk).wait_recv()
        link_out[chunk] = (kept[chunk, 1] + core_in[chunk, 1].astype(F32)).astype(BF16)
        to_link(chunk).start()

    def over_scan(chunk):
        to_link(chunk).wait_recv()
        for d in (1, 2, 0):
            total = kept[chunk, 0, d] + core_in[chunk, 0, d].astype(F32) + link_in[chunk, d].astype(F32)
            if d:
                scan_out[chunk, d - 1] = total.astype(BF16)
                to_scan(chunk, d - 1).start()
            else:
                near_ref[chunk * block_rows : (chunk + 1) * block_rows] = total

    def finish(chunk):
        rows = slice(chunk * block_rows, (chunk + 1) * block_rows)
        to_scan(chunk, 0).wait_recv()
        far_ref[rows] = scan_in[chunk, 0].astype(F32)
        to_scan(chunk, 1).wait_recv()
        near_ref[rows] += scan_in[chunk, 1].astype(F32)

    for chunk in range(chunks):
        compute(chunk)
        if chunk:
            over_link(chunk - 1)
    over_link(chunks - 1)
    for chunk in range(chunks):
        over_scan(chunk)
    for chunk in range(chunks):
        finish(chunk)
    for chunk in range(chunks):
        to_core(chunk).wait_send()
        to_link(chunk).wait_send()
        for which in range(2):
            to_scan(chunk, which).wait_send()


def forward(matrix, bounds, strip, shares, scan_size, block_rows=8):
    _, beams, strip_rows, window = strip.shape
    assert shares == 4 and scan_size > 4
    pairs = shares // 2
    group = matrix.shape[0] // (3 * shares)
    chunks = strip_rows // block_rows
    tail = (block_rows, group, window)
    vmem = pl.BlockSpec(memory_space=pltpu.VMEM)
    dma = pltpu.SemaphoreType.DMA
    return pl.pallas_call(
        functools.partial(forward_kernel, shares, scan_size),
        out_shape=[jax.ShapeDtypeStruct((strip_rows, group, window), F32)] * 2,
        in_specs=[vmem, vmem, pl.BlockSpec(memory_space=pl.ANY)],
        out_specs=[vmem, vmem],
        scratch_shapes=[
            pltpu.VMEM((2, 2, beams, block_rows, window), BF16),
            pltpu.VMEM((2 * beams * block_rows, window), F32),
            pltpu.VMEM((chunks, pairs, 3) + tail, F32),
            pltpu.VMEM((chunks, pairs, 3) + tail, BF16),
            pltpu.VMEM((chunks, pairs, 3) + tail, BF16),
            pltpu.VMEM((chunks, 3) + tail, BF16),
            pltpu.VMEM((chunks, 3) + tail, BF16),
            pltpu.VMEM((chunks, 2) + tail, BF16),
            pltpu.VMEM((chunks, 2) + tail, BF16),
            dma((2,)),
            dma((chunks,)),
            dma((chunks,)),
            dma((chunks,)),
            dma((chunks,)),
            dma((chunks, 2)),
            dma((chunks, 2)),
        ],
        compiler_params=pltpu.CompilerParams(
            collective_id=0, has_side_effects=True, vmem_limit_bytes=52 << 20
        ),
        cost_estimate=pl.CostEstimate(
            flops=2 * matrix.size * strip_rows * window,
            bytes_accessed=4 * beams * strip_rows * window,
            transcendentals=0,
        ),
    )(bounds, matrix, strip)


def backward_kernel(block_rows, bounds_ref, matrix_ref, parts_ref, out_ref, wide):
    depth = matrix_ref.shape[0]
    window = out_ref.shape[3]
    first = pl.program_id(0) * block_rows
    low = bounds_ref[0]
    high = bounds_ref[1]
    pieces = [
        (d, s, g)
        for d in range(parts_ref.shape[0])
        for s in range(parts_ref.shape[1])
        for g in range(parts_ref.shape[2])
    ]
    for row in range(0, block_rows, 2):
        sides = []
        for k in range(2):
            here = first + row + k
            inside = (low <= here) & (here < high)
            tall = jnp.concatenate([parts_ref[d, s, g, row + k] for d, s, g in pieces], axis=0)
            sides.append(jnp.where(inside, tall.astype(F32), 0.0).astype(BF16))
        sums = jnp.dot(
            matrix_ref[...], jnp.concatenate(sides, axis=1), preferred_element_type=F32
        )
        for k in range(2):
            wide[pl.ds(row + k, depth, stride=block_rows), :] = sums[:, k * window : (k + 1) * window]
    out_ref[...] = wide[...].reshape(out_ref.shape).astype(BF16)


def backward(matrix, bounds, parts, beams, block_rows=8):
    kinds, shares, groups, strip_rows, depth, window = parts.shape
    return pl.pallas_call(
        functools.partial(backward_kernel, block_rows),
        grid=(strip_rows // block_rows,),
        out_shape=jax.ShapeDtypeStruct((2, beams, strip_rows, window), BF16),
        in_specs=[
            pl.BlockSpec(bounds.shape, lambda i: (0, 0, 0)),
            pl.BlockSpec(matrix.shape, lambda i: (0, 0)),
            pl.BlockSpec(
                (kinds, shares, groups, block_rows, depth, window), lambda i: (0, 0, 0, i, 0, 0)
            ),
        ],
        out_specs=pl.BlockSpec((2, beams, block_rows, window), lambda i: (0, 0, i, 0)),
        scratch_shapes=[pltpu.VMEM((2 * beams * block_rows, window), F32)],
        compiler_params=pltpu.CompilerParams(vmem_limit_bytes=28 << 20),
        cost_estimate=pl.CostEstimate(
            flops=2 * matrix.size * strip_rows * window,
            bytes_accessed=4 * beams * strip_rows * window + 2 * parts.size,
            transcendentals=0,
        ),
    )(bounds, matrix, parts)


def three_products(left_high, left_low, right_high, right_low):
    total = jnp.dot(left_low, right_high, preferred_element_type=F32)
    total += jnp.dot(left_high, right_low, preferred_element_type=F32)
    return total + jnp.dot(left_high, right_high, preferred_element_type=F32)


def gradient_kernel(shares, scan_size, near_ref, far_ref, live_ref, tables_ref, amplitude_ref,
                    out_ref, measured, waves, backs, own_far, load_sem,
                    link_send, link_recv, scan_send, scan_recv, core_send, core_recv):
    _, _, groups, strip_rows, depth, window = out_ref.shape
    share = depth // 2
    rows = strip_rows * share
    half_rows = strip_rows // 2
    me = lax.axis_index("beam")
    tile = lax.axis_index("scan")
    core_mate = {"beam": me + 1 - 2 * lax.rem(me, 2)}
    link_mate = {"beam": lax.rem(me + shares // 2, shares)}
    owners = [{"scan": lax.rem(tile + d, scan_size)} for d in (1, 2)]
    givers = [{"scan": lax.rem(tile + scan_size - d, scan_size)} for d in (1, 2)]
    halves = [pl.ds(h * half_rows, half_rows) for h in range(2)]
    link_at = {(0, 0): 0, (0, 1): 1, (1, 0): 2, (1, 1): 3, (2, 0): 4}
    scan_at = {(1, 0, 0): 0, (1, 0, 1): 1, (2, 0, 0): 2, (2, 0, 1): 3, (2, 1, 1): 4}

    load = pltpu.make_async_copy(
        amplitude_ref.at[pl.ds(me * groups * share, groups * share)], measured, load_sem
    )
    load.start()

    def over_link(d, g, h):
        at = link_at[d, g]
        return pltpu.make_async_remote_copy(
            out_ref.at[d, 0, g, halves[h]], out_ref.at[d, 1, g, halves[h]],
            link_send.at[at, h], link_recv.at[at, h],
            device_id=link_mate, device_id_type=MESH,
        )

    def over_core(d, s, g, h):
        at = (d * 2 + s) * groups + g
        return pltpu.make_async_remote_copy(
            out_ref.at[d, s, g, halves[h]], out_ref.at[d, s + 2, g, halves[h]],
            core_send.at[at, h], core_recv.at[at, h],
            device_id=core_mate, device_id_type=MESH,
        )

    def over_scan(d, s, g, h):
        at = scan_at[d, s, g]
        source = own_far.at[g] if d == 1 else out_ref.at[0, s, g]
        return pltpu.make_async_remote_copy(
            source.at[halves[h]], out_ref.at[d, s, g, halves[h]],
            scan_send.at[at, h], scan_recv.at[at, h],
            device_id=owners[d - 1], device_id_type=MESH,
        )

    def by_columns(high, low, table):
        return three_products(high, low, tables_ref[table], tables_ref[table + 1])

    def transform(g):
        for half in range(2):
            block = (near_ref if half == 0 else far_ref)[:, g * depth : (g + 1) * depth, :]
            wide = jnp.concatenate(
                [block[:, :share].reshape(rows, window), block[:, share:].reshape(rows, window)], axis=1
            )
            high, low = split_two(wide)
            done = by_columns(high, low, 0)
            for c in range(2):
                waves[c, half * rows : (half + 1) * rows, :] = done[:, c * window : (c + 1) * window]

        for p in range(0, share, 2):
            columns = []
            for k in range(2):
                columns.append(
                    jnp.concatenate(
                        [waves[c, pl.ds(p + k, window, stride=share), :] for c in range(2)], axis=0
                    )
                )
            high, low = split_two(jnp.concatenate(columns, axis=1))
            far = three_products(tables_ref[4], tables_ref[5], high, low)
            far_re, far_im = far[:window], far[window:]
            at = g * share + p
            values = jnp.concatenate([measured[at], measured[at + 1]], axis=1)
            modulus = jnp.sqrt(far_re * far_re + far_im * far_im + ETA)
            keep_share = 1.0 - values / modulus
            high, low = split_two(jnp.concatenate([far_re * keep_share, far_im * keep_share], axis=0))
            back = three_products(tables_ref[6], tables_ref[7], high, low)
            for k in range(2):
                for c in range(2):
                    backs[c, pl.ds(p + k, window, stride=share), :] = back[
                        c * window : (c + 1) * window, k * window : (k + 1) * window
                    ]

        live = live_ref[g * share : (g + 1) * share][None]
        for half in (1, 0):
            wide = jnp.concatenate(
                [backs[c, half * rows : (half + 1) * rows, :] for c in range(2)], axis=1
            )
            high, low = split_two(wide)
            done = by_columns(high, low, 2)
            pieces = [
                done[:, c * window : (c + 1) * window].reshape(strip_rows, share, window) * live
                for c in range(2)
            ]
            value = jnp.concatenate(pieces, axis=1).astype(BF16)
            if half:
                own_far[g] = value
                for h in range(2):
                    over_scan(1, 0, g, h).start()
            else:
                out_ref[0, 0, g] = value
                for h in range(2):
                    over_link(0, g, h).start()
                    over_scan(2, 0, g, h).start()
                    over_core(0, 0, g, h).start()

    barrier = pltpu.get_barrier_semaphore()
    peers = [core_mate, link_mate] + owners + givers
    for peer in peers:
        pl.semaphore_signal(barrier, inc=1, device_id=peer, device_id_type=MESH)
    pl.semaphore_wait(barrier, len(peers))
    load.wait()
    for g in range(groups):
        transform(g)

    def got_scan(d, s, g, link):
        for h in range(2):
            over_scan(d, s, g, h).wait_recv()
            if link:
                over_link(d, g, h).start()
            over_core(d, s, g, h).start()

    def got_link(d, g, scan):
        for h in range(2):
            over_link(d, g, h).wait_recv()
            if scan:
                over_scan(2, 1, g, h).start()
            over_core(d, 1, g, h).start()

    got_scan(1, 0, 0, True)
    got_link(0, 0, False)
    got_scan(2, 0, 0, True)
    got_link(0, 1, True)
    got_scan(1, 0, 1, True)
    got_link(1, 0, False)
    got_scan(2, 0, 1, False)
    got_link(2, 0, False)
    got_scan(2, 1, 1, False)
    got_link(1, 1, False)
    for d in range(3):
        for s in range(2):
            for g in range(groups):
                for h in range(2):
                    over_core(d, s, g, h).wait()
    for d, g in link_at:
        for h in range(2):
            over_link(d, g, h).wait_send()
    for d, s, g in scan_at:
        for h in range(2):
            over_scan(d, s, g, h).wait_send()


def gradients(near, far, live, tables, amplitude, shares, scan_size, groups):
    strip_rows, depth, window = near.shape
    share_rows = depth // 2
    assert groups == 2 and shares == 4 and scan_size > 4
    tail = (strip_rows, depth // groups, window)
    vmem = pl.BlockSpec(memory_space=pltpu.VMEM)
    dma = pltpu.SemaphoreType.DMA
    return pl.pallas_call(
        functools.partial(gradient_kernel, shares, scan_size),
        out_shape=jax.ShapeDtypeStruct((3, shares, groups) + tail, BF16),
        in_specs=[vmem, vmem, vmem, vmem, pl.BlockSpec(memory_space=pl.ANY)],
        out_specs=vmem,
        scratch_shapes=[
            pltpu.VMEM((share_rows, window, window), F32),
            pltpu.VMEM((2, window * share_rows // groups, window), F32),
            pltpu.VMEM((2, window * share_rows // groups, window), F32),
            pltpu.VMEM((groups,) + tail, BF16),
            dma,
            dma((5, 2)),
            dma((5, 2)),
            dma((5, 2)),
            dma((5, 2)),
            dma((6 * groups, 2)),
            dma((6 * groups, 2)),
        ],
        compiler_params=pltpu.CompilerParams(
            collective_id=1, has_side_effects=True, vmem_limit_bytes=40 << 20
        ),
        cost_estimate=pl.CostEstimate(
            flops=24 * share_rows * 4 * window**3 * 2,
            bytes_accessed=16 * near.size,
            transcendentals=0,
        ),
    )(near, far, live, tables, amplitude)


def transform_tables(window):
    counter = np.arange(window)
    turn_angle = (counter[:, None] * counter[None, :] % window) * (2.0 * np.pi / window)
    table_re = np.cos(turn_angle) / np.sqrt(window)
    table_im = -np.sin(turn_angle) / np.sqrt(window)
    stacked = []
    for left in (False, True):
        for sign in (1.0, -1.0):
            imag = sign * table_im
            if left:
                full = np.block([[table_re, -imag], [imag, table_re]])
            else:
                full = np.block([[table_re, imag], [-imag, table_re]])
            high = full.astype(BF16)
            stacked += [high, (full - high.astype(np.float64)).astype(BF16)]
    return jnp.asarray(np.stack(stacked))


def share_order(shares):
    order = [0]
    bit = shares // 2
    while bit:
        order = order + [o | bit for o in order]
        bit //= 2
    return order


def body(smatrix, beam_freq, beam_amp, row_offset, col_offset, counts, amplitude):
    beam_dev = smatrix.shape[1]
    strip_rows = smatrix.shape[2]
    window = smatrix.shape[3]
    per_tile = row_offset.shape[0]
    scan_size = lax.axis_size("scan")
    shares = lax.axis_size("beam")
    share_rows = per_tile // shares
    field_rows = strip_rows * scan_size
    assert window == 2 * strip_rows
    my_tile = lax.axis_index("scan")
    my_beam = lax.axis_index("beam")
    order = share_order(shares)

    offsets = jnp.stack([row_offset, col_offset])
    offset_sets = [offsets] + [passed_along(offsets, "scan", d) for d in (1, 2)]
    stacked = jnp.stack(offset_sets).reshape(3, 2, shares, share_rows)
    stacked = jnp.take(stacked, jnp.array(order, jnp.int32) ^ my_beam, axis=2)
    rows = stacked[:, 0]
    cols = stacked[:, 1]
    distance = jnp.arange(3, dtype=jnp.int32)[:, None, None]
    tile_ids = (my_tile - distance) % scan_size
    coef_re, coef_im = coefficients(
        (tile_ids * strip_rows + rows).reshape(-1),
        cols.reshape(-1),
        beam_freq,
        beam_amp,
        field_rows,
        window,
    )
    real_rows = jnp.concatenate([coef_re, -coef_im], axis=1)
    imag_rows = jnp.concatenate([coef_im, coef_re], axis=1)
    split = (3 * shares * GROUPS, share_rows // GROUPS, 2 * beam_dev)
    matrix = jnp.stack(
        [real_rows.reshape(split), imag_rows.reshape(split)], axis=1
    ).reshape(6 * per_tile, 2 * beam_dev)
    low = jnp.where(distance == 0, rows, 0)
    high = jnp.where(distance == 2, rows, strip_rows)
    split = (2, 3, shares, GROUPS, 2, share_rows // GROUPS)
    bounds = jnp.stack([low, high]).reshape(split[:4] + (1,) + split[5:])
    bounds = jnp.broadcast_to(bounds, split).reshape(2, 6 * per_tile, 1)
    bounds = jnp.broadcast_to(bounds, (2, 6 * per_tile, window))
    first_row = my_beam * share_rows
    live = (first_row + jnp.arange(share_rows, dtype=jnp.int32) < counts[0]).astype(F32)
    live = jnp.broadcast_to(live[:, None], (share_rows, window))
    tables = transform_tables(window)

    near, far = forward(matrix, bounds, smatrix, shares, scan_size)
    parts = gradients(near, far, live, tables, amplitude, shares, scan_size, GROUPS)
    return backward(matrix.T, bounds, parts, beam_dev)


def solution(mesh):
    return jax.shard_map(
        body,
        mesh=mesh,
        in_specs=(
            P(None, "beam", "scan", None),
            P(None, "beam"),
            P(None, "beam"),
            P("scan"),
            P("scan"),
            P("scan"),
            P("scan", None, None),
        ),
        out_specs=P(None, "beam", "scan", None),
        check_vma=False,
    )
```

```python
import functools

import jax
import jax.numpy as jnp
import numpy as np
from jax import lax
from jax.experimental import pallas as pl
from jax.experimental.pallas import tpu as pltpu
from jax.sharding import PartitionSpec as P

TWO_PI = 6.283185307179586
ETA = 0.1
F32 = jnp.float32
BF16 = jnp.bfloat16
MESH = pl.DeviceIdType.MESH


def split_two(value):
    high = value.astype(BF16)
    return high, (value - high.astype(F32)).astype(BF16)


def three_products(left_high, left_low, right_high, right_low):
    total = jnp.dot(left_low, right_high, preferred_element_type=F32)
    total += jnp.dot(left_high, right_low, preferred_element_type=F32)
    return total + jnp.dot(left_high, right_high, preferred_element_type=F32)


def wave_kernel(shares, scan_size, spots_ref, freq_ref, amp_ref, live_ref, tables_ref, strip_ref,
                amplitude_ref, parts_ref, matrix_ref, offset_ref,
                spots, strips, wide, kept, core_out, core_in, link_out, link_in, zed_out, zed_in,
                scan_out, scan_in, near, far, measured, waves, backs, own_far,
                load_sem, amp_sem, spot_send, spot_recv, pair_send, pair_recv, link_send, link_recv,
                zed_send, zed_recv, scan_send, scan_recv,
                hop_send, hop_recv, step_send, step_recv, join_send, join_recv):
    chunks, pairs, _, block_rows, group, window = kept.shape
    _, _, groups, strip_rows, depth, _ = parts_ref.shape
    beams = strip_ref.shape[1]
    share = depth // 2
    share_rows = group // 2
    field_rows = strip_rows * scan_size
    me = lax.axis_index("beam")
    tile = lax.axis_index("scan")
    core_id = me + 1 - 2 * lax.rem(me, 2)
    core_mate = {"beam": core_id}
    link_mate = {"beam": lax.rem(me + pairs, shares)}
    share_ids = [me, lax.rem(me + pairs, shares), core_id, lax.rem(core_id + pairs, shares)]
    before = [{"scan": lax.rem(tile + scan_size - d, scan_size)} for d in (1, 2)]
    after = [{"scan": lax.rem(tile + d, scan_size)} for d in (1, 2)]

    def load(chunk):
        return pltpu.make_async_copy(
            strip_ref.at[:, :, pl.ds(chunk * block_rows, block_rows), :],
            strips.at[chunk % 2],
            load_sem.at[chunk % 2],
        )

    def remote(source, target, sends, recvs, device):
        return pltpu.make_async_remote_copy(
            source, target, sends, recvs, device_id=device, device_id_type=MESH
        )

    def spot_copy(d):
        return remote(spots_ref, spots.at[d - 1], spot_send.at[d - 1], spot_recv.at[d - 1], after[d - 1])

    load(0).start()
    load(1).start()
    load_amplitude = pltpu.make_async_copy(
        amplitude_ref.at[pl.ds(me * share_rows, share_rows)], measured, amp_sem
    )
    load_amplitude.start()
    barrier = pltpu.get_barrier_semaphore()
    peers = [core_mate, link_mate] + before + after
    for peer in peers:
        pl.semaphore_signal(barrier, inc=1, device_id=peer, device_id_type=MESH)
    pl.semaphore_wait(barrier, len(peers))
    spot_copy(1).start()
    spot_copy(2).start()

    def coefficients(d):
        source = spots_ref if d == 0 else spots.at[d - 1]
        tile_id = lax.rem(tile + scan_size - d, scan_size)
        for s in range(shares):
            here = pl.ds(share_ids[s] * share_rows, share_rows)
            rows = source[0, here, :]
            cols = source[1, here, :]
            base = (d * shares + s) * group
            if d != 1:
                at = s * group
                for g in range(groups):
                    own = rows[g * share : (g + 1) * share]
                    offset_ref[d // 2, at + g * depth : at + (g + 1) * depth, :] = jnp.concatenate(
                        [own, own], axis=0
                    )
            for lane in range(0, beams, window):
                lanes = slice(lane, lane + window)
                along_rows = (freq_ref[0:1, lanes] * (tile_id * strip_rows + rows)) & (field_rows - 1)
                along_cols = (freq_ref[1:2, lanes] * cols) & (window - 1)
                turns = along_rows.astype(F32) / field_rows + along_cols.astype(F32) / window
                angle = -TWO_PI * turns
                cos_part = jnp.cos(angle)
                sin_part = jnp.sin(angle)
                coef_re = amp_ref[0:1, lanes] * cos_part - amp_ref[1:2, lanes] * sin_part
                coef_im = amp_ref[0:1, lanes] * sin_part + amp_ref[1:2, lanes] * cos_part
                for g in range(groups):
                    re = coef_re[g * share : (g + 1) * share]
                    im = coef_im[g * share : (g + 1) * share]
                    spot = slice(base + g * depth, base + (g + 1) * depth)
                    matrix_ref[spot, lanes] = jnp.concatenate([re, im], axis=0).astype(BF16)
                    matrix_ref[spot, beams + lane : beams + lane + window] = jnp.concatenate(
                        [-im, re], axis=0
                    ).astype(BF16)

    coefficients(0)
    for d in (1, 2):
        spot_copy(d).wait()
        coefficients(d)

    def to_core(chunk):
        return remote(
            core_out.at[chunk], core_in.at[chunk], pair_send.at[chunk], pair_recv.at[chunk], core_mate
        )

    def to_link(g, chunk, late):
        if chunk >= chunks // 2:
            pieces = slice(0, 3)
        elif late:
            pieces = slice(0, 1)
        else:
            pieces = slice(1, 2)
        pieces = pl.ds(pieces.start, pieces.stop - pieces.start)
        return remote(
            link_out.at[g, chunk, pieces], link_in.at[g, chunk, pieces],
            link_send.at[g, chunk, late], link_recv.at[g, chunk, late], link_mate,
        )

    def to_zed(g, chunk):
        return remote(
            zed_out.at[g, chunk], zed_in.at[g, chunk],
            zed_send.at[g, chunk], zed_recv.at[g, chunk], before[1],
        )

    def to_scan(g, chunk, which):
        return remote(
            scan_out.at[g, chunk, which], scan_in.at[g, chunk, which],
            scan_send.at[g, chunk, which], scan_recv.at[g, chunk, which], before[which],
        )

    def compute(chunk):
        load(chunk).wait()
        wide[...] = strips[chunk % 2].astype(F32).reshape(2 * beams * block_rows, window)
        if chunk + 2 < chunks:
            load(chunk + 2).start()

        def pair_of_rows(step, carry):
            row = step * 2
            rhs = jnp.concatenate(
                [wide[pl.ds(row + k, 2 * beams, stride=block_rows), :] for k in range(2)], axis=1
            ).astype(BF16)
            sums = jnp.dot(matrix_ref[...], rhs, preferred_element_type=F32)
            for k in range(2):
                here = chunk * block_rows + row + k
                for d in range(3):
                    for s in range(shares):
                        at = (d * shares + s) * group
                        piece = sums[at : at + group, k * window : (k + 1) * window]
                        if d == 0:
                            piece = jnp.where(here >= offset_ref[0, s * group : (s + 1) * group], piece, 0.0)
                        if d == 2:
                            piece = jnp.where(here < offset_ref[1, s * group : (s + 1) * group], piece, 0.0)
                        if s < pairs:
                            kept[chunk, s, d, row + k] = piece
                        else:
                            core_out[chunk, s - pairs, d, row + k] = piece.astype(BF16)
            return carry

        lax.fori_loop(0, block_rows // 2, pair_of_rows, 0)
        to_core(chunk).start()

    def held(g, chunk, s, d):
        part = slice(g * depth, (g + 1) * depth)
        return kept[chunk, s, d, :, part, :] + core_in[chunk, s, d, :, part, :].astype(F32)

    def after_core(g, chunk):
        if g == 0:
            to_core(chunk).wait_recv()
        link_out[g, chunk, 1] = held(g, chunk, 1, 1).astype(BF16)
        if chunk < chunks // 2:
            for s in range(2):
                zed_out[g, chunk, s] = held(g, chunk, s, 2).astype(BF16)
            to_zed(g, chunk).start()
        else:
            for d in (0, 2):
                link_out[g, chunk, d] = held(g, chunk, 1, d).astype(BF16)
        to_link(g, chunk, 0).start()

    def after_zed(g, chunk):
        to_zed(g, chunk).wait_recv()
        link_out[g, chunk, 0] = (held(g, chunk, 1, 0) + zed_in[g, chunk, 1].astype(F32)).astype(BF16)
        to_link(g, chunk, 1).start()

    def rows_of(chunk):
        return slice(chunk * block_rows, (chunk + 1) * block_rows)

    def after_link(g, chunk):
        to_link(g, chunk, 0).wait_recv()
        for d in (1, 2) if chunk >= chunks // 2 else (1,):
            scan_out[g, chunk, d - 1] = (
                held(g, chunk, 0, d) + link_in[g, chunk, d].astype(F32)
            ).astype(BF16)
            to_scan(g, chunk, d - 1).start()
        if chunk >= chunks // 2:
            near[g, rows_of(chunk)] = held(g, chunk, 0, 0) + link_in[g, chunk, 0].astype(F32)

    def finish(g, chunk):
        if chunk < chunks // 2:
            to_link(g, chunk, 1).wait_recv()
            near[g, rows_of(chunk)] = (
                held(g, chunk, 0, 0)
                + zed_in[g, chunk, 0].astype(F32)
                + link_in[g, chunk, 0].astype(F32)
            )
        to_scan(g, chunk, 0).wait_recv()
        far[g, rows_of(chunk)] = scan_in[g, chunk, 0].astype(F32)
        if chunk >= chunks // 2:
            to_scan(g, chunk, 1).wait_recv()
            near[g, rows_of(chunk)] += scan_in[g, chunk, 1].astype(F32)

    half_rows = strip_rows // 2
    halves = [pl.ds(h * half_rows, half_rows) for h in range(2)]
    hop_at = {(0, 0): 0, (0, 1): 1, (1, 0): 2, (1, 1): 3, (2, 0): 4}
    step_at = {(1, 0, 0): 0, (1, 0, 1): 1, (2, 0, 0): 2, (2, 0, 1): 3, (2, 1, 1): 4}

    def over_link(d, g, h):
        at = hop_at[d, h]
        return remote(
            parts_ref.at[d, 0, g, halves[h]], parts_ref.at[d, 1, g, halves[h]],
            hop_send.at[g, at], hop_recv.at[g, at], link_mate,
        )

    def over_core(d, s, g, h):
        at = d * 2 + s
        return remote(
            parts_ref.at[d, s, g, halves[h]], parts_ref.at[d, s + 2, g, halves[h]],
            join_send.at[g, at, h], join_recv.at[g, at, h], core_mate,
        )

    def over_scan(d, s, g, h):
        at = step_at[d, s, h]
        source = own_far.at[g] if d == 1 else parts_ref.at[0, s, g]
        return remote(
            source.at[halves[h]], parts_ref.at[d, s, g, halves[h]],
            step_send.at[g, at], step_recv.at[g, at], after[d - 1],
        )

    def by_columns(high, low, table):
        return three_products(high, low, tables_ref[table], tables_ref[table + 1])

    def transform(g):
        rows = strip_rows * share
        for half in range(2):
            block = (near if half == 0 else far)[g]
            tall = jnp.concatenate(
                [block[:, :share].reshape(rows, window), block[:, share:].reshape(rows, window)], axis=1
            )
            high, low = split_two(tall)
            done = by_columns(high, low, 0)
            for c in range(2):
                waves[c, half * rows : (half + 1) * rows, :] = done[:, c * window : (c + 1) * window]

        for p in range(0, share, 2):
            columns = []
            for k in range(2):
                columns.append(
                    jnp.concatenate(
                        [waves[c, pl.ds(p + k, window, stride=share), :] for c in range(2)], axis=0
                    )
                )
            high, low = split_two(jnp.concatenate(columns, axis=1))
            wave = three_products(tables_ref[4], tables_ref[5], high, low)
            wave_re, wave_im = wave[:window], wave[window:]
            at = g * share + p
            values = jnp.concatenate([measured[at], measured[at + 1]], axis=1)
            modulus = jnp.sqrt(wave_re * wave_re + wave_im * wave_im + ETA)
            keep_share = 1.0 - values / modulus
            high, low = split_two(jnp.concatenate([wave_re * keep_share, wave_im * keep_share], axis=0))
            back = three_products(tables_ref[6], tables_ref[7], high, low)
            for k in range(2):
                for c in range(2):
                    backs[c, pl.ds(p + k, window, stride=share), :] = back[
                        c * window : (c + 1) * window, k * window : (k + 1) * window
                    ]

        live = live_ref[g * share : (g + 1) * share][None]
        for half in (1, 0):
            tall = jnp.concatenate(
                [backs[c, half * rows : (half + 1) * rows, :] for c in range(2)], axis=1
            )
            high, low = split_two(tall)
            done = by_columns(high, low, 2)
            pieces = [
                done[:, c * window : (c + 1) * window].reshape(strip_rows, share, window) * live
                for c in range(2)
            ]
            value = jnp.concatenate(pieces, axis=1).astype(BF16)
            if half:
                own_far[g] = value
                for h in range(2):
                    over_scan(1, 0, g, h).start()
            else:
                parts_ref[0, 0, g] = value
                for h in (1, 0):
                    over_link(0, g, h).start()
                for h in range(2):
                    over_scan(2, 0, g, h).start()
                    over_core(0, 0, g, h).start()

    def got_scan(d, s, g, h, link):
        over_scan(d, s, g, h).wait_recv()
        if link:
            over_link(d, g, h).start()
        over_core(d, s, g, h).start()

    def got_link(d, g, h, scan):
        over_link(d, g, h).wait_recv()
        if scan:
            over_scan(2, 1, g, h).start()
        over_core(d, 1, g, h).start()

    def relay(g):
        got_scan(1, 0, g, 0, True)
        got_scan(1, 0, g, 1, True)
        got_link(0, g, 1, True)
        got_link(0, g, 0, False)
        got_scan(2, 0, g, 0, True)
        got_scan(2, 0, g, 1, False)
        got_link(1, g, 0, False)
        got_link(1, g, 1, False)
        got_scan(2, 1, g, 1, False)
        got_link(2, g, 0, False)

    early = range(chunks // 2)
    for chunk in range(chunks):
        compute(chunk)
        if chunk:
            after_core(0, chunk - 1)
    after_core(0, chunks - 1)
    for chunk in early:
        after_zed(0, chunk)
    for chunk in range(chunks):
        after_core(1, chunk)
    for chunk in range(chunks):
        after_link(0, chunk)
    for chunk in early:
        after_zed(1, chunk)
    for chunk in range(chunks):
        finish(0, chunk)
    load_amplitude.wait()
    transform(0)
    for chunk in range(chunks):
        after_link(1, chunk)
    for chunk in range(chunks):
        finish(1, chunk)
    transform(1)
    for g in range(groups):
        relay(g)

    for chunk in range(chunks):
        to_core(chunk).wait_send()
        for g in range(groups):
            to_link(g, chunk, 0).wait_send()
            to_scan(g, chunk, 0).wait_send()
            if chunk < chunks // 2:
                to_link(g, chunk, 1).wait_send()
                to_zed(g, chunk).wait_send()
            else:
                to_scan(g, chunk, 1).wait_send()
    for g in range(groups):
        for d in range(3):
            for s in range(2):
                for h in range(2):
                    over_core(d, s, g, h).wait()
        for d, h in hop_at:
            over_link(d, g, h).wait_send()
        for d, s, h in step_at:
            over_scan(d, s, g, h).wait_send()


def waves_to_gradients(spots, freq, amp, live, tables, strip, amplitude, shares, scan_size,
                       groups=2, block_rows=8):
    _, beams, strip_rows, window = strip.shape
    per_tile = spots.shape[1]
    share_rows = per_tile // shares
    group = 2 * share_rows
    depth = group // groups
    field_rows = strip_rows * scan_size
    chunks = strip_rows // block_rows
    pairs = shares // 2
    assert groups == 2 and shares == 4 and scan_size > 4 and chunks % 2 == 0
    assert field_rows & (field_rows - 1) == 0 and window & (window - 1) == 0
    tail = (block_rows, depth, window)
    vmem = pl.BlockSpec(memory_space=pltpu.VMEM)
    anywhere = pl.BlockSpec(memory_space=pl.ANY)
    dma = pltpu.SemaphoreType.DMA
    return pl.pallas_call(
        functools.partial(wave_kernel, shares, scan_size),
        out_shape=[
            jax.ShapeDtypeStruct((3, shares, groups, strip_rows, depth, window), BF16),
            jax.ShapeDtypeStruct((3 * shares * group, 2 * beams), BF16),
            jax.ShapeDtypeStruct((2, shares * group, window), jnp.int32),
        ],
        in_specs=[vmem] * 5 + [anywhere] * 2,
        out_specs=[vmem] * 3,
        scratch_shapes=[
            pltpu.VMEM((2, 2, per_tile, window), jnp.int32),
            pltpu.VMEM((2, 2, beams, block_rows, window), BF16),
            pltpu.VMEM((2 * beams * block_rows, window), F32),
            pltpu.VMEM((chunks, pairs, 3, block_rows, group, window), F32),
            pltpu.VMEM((chunks, pairs, 3, block_rows, group, window), BF16),
            pltpu.VMEM((chunks, pairs, 3, block_rows, group, window), BF16),
            pltpu.VMEM((groups, chunks, 3) + tail, BF16),
            pltpu.VMEM((groups, chunks, 3) + tail, BF16),
            pltpu.VMEM((groups, chunks // 2, 2) + tail, BF16),
            pltpu.VMEM((groups, chunks // 2, 2) + tail, BF16),
            pltpu.VMEM((groups, chunks, 2) + tail, BF16),
            pltpu.VMEM((groups, chunks, 2) + tail, BF16),
            pltpu.VMEM((groups, strip_rows, depth, window), F32),
            pltpu.VMEM((groups, strip_rows, depth, window), F32),
            pltpu.VMEM((share_rows, window, window), F32),
            pltpu.VMEM((2, window * share_rows // groups, window), F32),
            pltpu.VMEM((2, window * share_rows // groups, window), F32),
            pltpu.VMEM((groups, strip_rows, depth, window), BF16),
            dma((2,)),
            dma,
            dma((2,)),
            dma((2,)),
            dma((chunks,)),
            dma((chunks,)),
            dma((groups, chunks, 2)),
            dma((groups, chunks, 2)),
            dma((groups, chunks // 2)),
            dma((groups, chunks // 2)),
            dma((groups, chunks, 2)),
            dma((groups, chunks, 2)),
            dma((groups, 5)),
            dma((groups, 5)),
            dma((groups, 5)),
            dma((groups, 5)),
            dma((groups, 6, 2)),
            dma((groups, 6, 2)),
        ],
        compiler_params=pltpu.CompilerParams(
            collective_id=0, has_side_effects=True, vmem_limit_bytes=48 << 20
        ),
        cost_estimate=pl.CostEstimate(
            flops=12 * per_tile * beams * strip_rows * window,
            bytes_accessed=4 * beams * strip_rows * window,
            transcendentals=0,
        ),
    )(spots, freq, amp, live, tables, strip, amplitude)


def backward_kernel(block_rows, offset_ref, matrix_ref, parts_ref, out_ref, wide):
    depth = matrix_ref.shape[0]
    window = out_ref.shape[3]
    first = pl.program_id(0) * block_rows
    kinds, shares, groups = parts_ref.shape[:3]
    for row in range(0, block_rows, 2):
        sides = []
        for k in range(2):
            here = first + row + k
            strips = []
            for d in range(kinds):
                tall = jnp.concatenate(
                    [parts_ref[d, s, g, row + k] for s in range(shares) for g in range(groups)], axis=0
                )
                if d == 0:
                    tall = jnp.where(here >= offset_ref[0], tall.astype(F32), 0.0).astype(BF16)
                if d == 2:
                    tall = jnp.where(here < offset_ref[1], tall.astype(F32), 0.0).astype(BF16)
                strips.append(tall)
            sides.append(jnp.concatenate(strips, axis=0))
        sums = jnp.dot(
            matrix_ref[...], jnp.concatenate(sides, axis=1), preferred_element_type=F32
        )
        for k in range(2):
            wide[pl.ds(row + k, depth, stride=block_rows), :] = sums[:, k * window : (k + 1) * window]
    out_ref[...] = wide[...].reshape(out_ref.shape).astype(BF16)


def backward(matrix, offsets, parts, beams, block_rows=8):
    kinds, shares, groups, strip_rows, depth, window = parts.shape
    return pl.pallas_call(
        functools.partial(backward_kernel, block_rows),
        grid=(strip_rows // block_rows,),
        out_shape=jax.ShapeDtypeStruct((2, beams, strip_rows, window), BF16),
        in_specs=[
            pl.BlockSpec(offsets.shape, lambda i: (0, 0, 0)),
            pl.BlockSpec(matrix.shape, lambda i: (0, 0)),
            pl.BlockSpec(
                (kinds, shares, groups, block_rows, depth, window), lambda i: (0, 0, 0, i, 0, 0)
            ),
        ],
        out_specs=pl.BlockSpec((2, beams, block_rows, window), lambda i: (0, 0, i, 0)),
        scratch_shapes=[pltpu.VMEM((2 * beams * block_rows, window), F32)],
        compiler_params=pltpu.CompilerParams(vmem_limit_bytes=28 << 20),
        cost_estimate=pl.CostEstimate(
            flops=2 * matrix.size * strip_rows * window,
            bytes_accessed=4 * beams * strip_rows * window + 2 * parts.size,
            transcendentals=0,
        ),
    )(offsets, matrix, parts)


def transform_tables(window):
    counter = np.arange(window)
    turn_angle = (counter[:, None] * counter[None, :] % window) * (2.0 * np.pi / window)
    table_re = np.cos(turn_angle) / np.sqrt(window)
    table_im = -np.sin(turn_angle) / np.sqrt(window)
    stacked = []
    for left in (False, True):
        for sign in (1.0, -1.0):
            imag = sign * table_im
            if left:
                full = np.block([[table_re, -imag], [imag, table_re]])
            else:
                full = np.block([[table_re, imag], [-imag, table_re]])
            high = full.astype(BF16)
            stacked += [high, (full - high.astype(np.float64)).astype(BF16)]
    return jnp.asarray(np.stack(stacked))


def body(smatrix, beam_freq, beam_amp, row_offset, col_offset, counts, amplitude):
    beam_dev = smatrix.shape[1]
    window = smatrix.shape[3]
    per_tile = row_offset.shape[0]
    scan_size = lax.axis_size("scan")
    shares = lax.axis_size("beam")
    share_rows = per_tile // shares
    assert window == 2 * smatrix.shape[2]
    spots = jnp.broadcast_to(
        jnp.stack([row_offset, col_offset])[:, :, None], (2, per_tile, window)
    )
    first_row = lax.axis_index("beam") * share_rows
    live = (first_row + jnp.arange(share_rows, dtype=jnp.int32) < counts[0]).astype(F32)
    live = jnp.broadcast_to(live[:, None], (share_rows, window))
    parts, matrix, offsets = waves_to_gradients(
        spots, beam_freq, beam_amp, live, transform_tables(window), smatrix, amplitude, shares, scan_size
    )
    return backward(matrix.T, offsets, parts, beam_dev)


def solution(mesh):
    return jax.shard_map(
        body,
        mesh=mesh,
        in_specs=(
            P(None, "beam", "scan", None),
            P(None, "beam"),
            P(None, "beam"),
            P("scan"),
            P("scan"),
            P("scan"),
            P("scan", None, None),
        ),
        out_specs=P(None, "beam", "scan", None),
        check_vma=False,
    )
```

```python
import functools

import jax
import jax.numpy as jnp
import numpy as np
from jax import lax
from jax.experimental import pallas as pl
from jax.experimental.pallas import tpu as pltpu
from jax.sharding import PartitionSpec as P

TWO_PI = 6.283185307179586
ETA = 0.1
F32 = jnp.float32
BF16 = jnp.bfloat16
MESH = pl.DeviceIdType.MESH


def split_two(value):
    high = value.astype(BF16)
    return high, (value - high.astype(F32)).astype(BF16)


def three_products(left_high, left_low, right_high, right_low):
    total = jnp.dot(left_low, right_high, preferred_element_type=F32)
    total += jnp.dot(left_high, right_low, preferred_element_type=F32)
    return total + jnp.dot(left_high, right_high, preferred_element_type=F32)


def wave_kernel(shares, scan_size, spots_ref, live_ref, freq_hbm, amp_hbm, tables_hbm, strip_ref,
                amplitude_ref, parts_ref, turned_ref, offset_ref,
                matrix_ref, freq_ref, amp_ref, tables_ref, spots, strips, wide, kept, core_out, core_in, link_out, link_in, zed_out, zed_in,
                scan_out, scan_in, near, far, measured, waves, backs, own_far,
                load_sem, side_sem, spot_send, spot_recv, pair_send, pair_recv, link_send, link_recv,
                zed_send, zed_recv, scan_send, scan_recv,
                hop_send, hop_recv, step_send, step_recv, join_send, join_recv):
    chunks, pairs, _, block_rows, group, window = kept.shape
    _, _, groups, strip_rows, depth, _ = parts_ref.shape
    beams = strip_ref.shape[1]
    share = depth // 2
    share_rows = group // 2
    field_rows = strip_rows * scan_size
    me = lax.axis_index("beam")
    tile = lax.axis_index("scan")
    core_id = me + 1 - 2 * lax.rem(me, 2)
    core_mate = {"beam": core_id}
    link_mate = {"beam": lax.rem(me + pairs, shares)}
    share_ids = [me, lax.rem(me + pairs, shares), core_id, lax.rem(core_id + pairs, shares)]
    before = [{"scan": lax.rem(tile + scan_size - d, scan_size)} for d in (1, 2)]
    after = [{"scan": lax.rem(tile + d, scan_size)} for d in (1, 2)]

    def load(chunk):
        return pltpu.make_async_copy(
            strip_ref.at[:, :, pl.ds(chunk * block_rows, block_rows), :],
            strips.at[chunk % 2],
            load_sem.at[chunk % 2],
        )

    def remote(source, target, sends, recvs, device):
        return pltpu.make_async_remote_copy(
            source, target, sends, recvs, device_id=device, device_id_type=MESH
        )

    def spot_copy(d):
        return remote(spots_ref, spots.at[d - 1], spot_send.at[d - 1], spot_recv.at[d - 1], after[d - 1])

    side_loads = [
        pltpu.make_async_copy(source, target, side_sem.at[i])
        for i, (source, target) in enumerate(
            [
                (freq_hbm, freq_ref),
                (amp_hbm, amp_ref),
                (tables_hbm, tables_ref),
                (amplitude_ref.at[pl.ds(me * share_rows, share_rows)], measured),
            ]
        )
    ]
    side_loads[0].start()
    side_loads[1].start()
    load(0).start()
    load(1).start()
    side_loads[2].start()
    side_loads[3].start()
    barrier = pltpu.get_barrier_semaphore()
    peers = [core_mate, link_mate] + before + after
    for peer in peers:
        pl.semaphore_signal(barrier, inc=1, device_id=peer, device_id_type=MESH)
    pl.semaphore_wait(barrier, len(peers))
    spot_copy(1).start()
    spot_copy(2).start()

    def coefficients(d):
        source = spots_ref if d == 0 else spots.at[d - 1]
        tile_id = lax.rem(tile + scan_size - d, scan_size)
        for s in range(shares):
            here = pl.ds(share_ids[s] * share_rows, share_rows)
            rows = source[0, here, :]
            cols = source[1, here, :]
            base = (d * shares + s) * group
            if d != 1:
                at = s * group
                for g in range(groups):
                    own = rows[g * share : (g + 1) * share]
                    offset_ref[d // 2, at + g * depth : at + (g + 1) * depth, :] = jnp.concatenate(
                        [own, own], axis=0
                    )
            for lane in range(0, beams, window):
                lanes = slice(lane, lane + window)
                along_rows = (freq_ref[0:1, lanes] * (tile_id * strip_rows + rows)) & (field_rows - 1)
                along_cols = (freq_ref[1:2, lanes] * cols) & (window - 1)
                turns = along_rows.astype(F32) / field_rows + along_cols.astype(F32) / window
                angle = -TWO_PI * turns
                cos_part = jnp.cos(angle)
                sin_part = jnp.sin(angle)
                coef_re = amp_ref[0:1, lanes] * cos_part - amp_ref[1:2, lanes] * sin_part
                coef_im = amp_ref[0:1, lanes] * sin_part + amp_ref[1:2, lanes] * cos_part
                for g in range(groups):
                    re = coef_re[g * share : (g + 1) * share]
                    im = coef_im[g * share : (g + 1) * share]
                    spot = slice(base + g * depth, base + (g + 1) * depth)
                    matrix_ref[spot, lanes] = jnp.concatenate([re, im], axis=0).astype(BF16)
                    matrix_ref[spot, beams + lane : beams + lane + window] = jnp.concatenate(
                        [-im, re], axis=0
                    ).astype(BF16)

    side_loads[0].wait()
    side_loads[1].wait()
    coefficients(0)
    for d in (1, 2):
        spot_copy(d).wait()
        coefficients(d)

    def to_core(chunk):
        return remote(
            core_out.at[chunk], core_in.at[chunk], pair_send.at[chunk], pair_recv.at[chunk], core_mate
        )

    def to_link(g, chunk, late):
        if chunk >= chunks // 2:
            pieces = slice(0, 3)
        elif late:
            pieces = slice(0, 1)
        else:
            pieces = slice(1, 2)
        pieces = pl.ds(pieces.start, pieces.stop - pieces.start)
        return remote(
            link_out.at[g, chunk, pieces], link_in.at[g, chunk, pieces],
            link_send.at[g, chunk, late], link_recv.at[g, chunk, late], link_mate,
        )

    def to_zed(g, chunk):
        return remote(
            zed_out.at[g, chunk], zed_in.at[g, chunk],
            zed_send.at[g, chunk], zed_recv.at[g, chunk], before[1],
        )

    def to_scan(g, chunk, which):
        return remote(
            scan_out.at[g, chunk, which], scan_in.at[g, chunk, which],
            scan_send.at[g, chunk, which], scan_recv.at[g, chunk, which], before[which],
        )

    def compute(chunk):
        load(chunk).wait()
        wide[...] = strips[chunk % 2].astype(F32).reshape(2 * beams * block_rows, window)
        if chunk + 2 < chunks:
            load(chunk + 2).start()

        def pair_of_rows(step, carry):
            row = step * 2
            rhs = jnp.concatenate(
                [wide[pl.ds(row + k, 2 * beams, stride=block_rows), :] for k in range(2)], axis=1
            ).astype(BF16)
            sums = jnp.dot(matrix_ref[...], rhs, preferred_element_type=F32)
            for k in range(2):
                here = chunk * block_rows + row + k
                for d in range(3):
                    for s in range(shares):
                        at = (d * shares + s) * group
                        piece = sums[at : at + group, k * window : (k + 1) * window]
                        if d == 0:
                            piece = jnp.where(here >= offset_ref[0, s * group : (s + 1) * group], piece, 0.0)
                        if d == 2:
                            piece = jnp.where(here < offset_ref[1, s * group : (s + 1) * group], piece, 0.0)
                        if s < pairs:
                            kept[chunk, s, d, row + k] = piece
                        else:
                            core_out[chunk, s - pairs, d, row + k] = piece.astype(BF16)
            return carry

        lax.fori_loop(0, block_rows // 2, pair_of_rows, 0)
        to_core(chunk).start()

    def held(g, chunk, s, d):
        part = slice(g * depth, (g + 1) * depth)
        return kept[chunk, s, d, :, part, :] + core_in[chunk, s, d, :, part, :].astype(F32)

    def after_core(g, chunk):
        if g == 0:
            to_core(chunk).wait_recv()
        link_out[g, chunk, 1] = held(g, chunk, 1, 1).astype(BF16)
        if chunk < chunks // 2:
            for s in range(2):
                zed_out[g, chunk, s] = held(g, chunk, s, 2).astype(BF16)
            to_zed(g, chunk).start()
        else:
            for d in (0, 2):
                link_out[g, chunk, d] = held(g, chunk, 1, d).astype(BF16)
        to_link(g, chunk, 0).start()

    def after_zed(g, chunk):
        to_zed(g, chunk).wait_recv()
        link_out[g, chunk, 0] = (held(g, chunk, 1, 0) + zed_in[g, chunk, 1].astype(F32)).astype(BF16)
        to_link(g, chunk, 1).start()

    def rows_of(chunk):
        return slice(chunk * block_rows, (chunk + 1) * block_rows)

    def after_link(g, chunk):
        to_link(g, chunk, 0).wait_recv()
        for d in (1, 2) if chunk >= chunks // 2 else (1,):
            scan_out[g, chunk, d - 1] = (
                held(g, chunk, 0, d) + link_in[g, chunk, d].astype(F32)
            ).astype(BF16)
            to_scan(g, chunk, d - 1).start()
        if chunk >= chunks // 2:
            near[g, rows_of(chunk)] = held(g, chunk, 0, 0) + link_in[g, chunk, 0].astype(F32)

    def finish(g, chunk):
        if chunk < chunks // 2:
            to_link(g, chunk, 1).wait_recv()
            near[g, rows_of(chunk)] = (
                held(g, chunk, 0, 0)
                + zed_in[g, chunk, 0].astype(F32)
                + link_in[g, chunk, 0].astype(F32)
            )
        to_scan(g, chunk, 0).wait_recv()
        far[g, rows_of(chunk)] = scan_in[g, chunk, 0].astype(F32)
        if chunk >= chunks // 2:
            to_scan(g, chunk, 1).wait_recv()
            near[g, rows_of(chunk)] += scan_in[g, chunk, 1].astype(F32)

    half_rows = strip_rows // 2
    halves = [pl.ds(h * half_rows, half_rows) for h in range(2)]
    hop_at = {(0, 0): 0, (0, 1): 1, (1, 0): 2, (1, 1): 3, (2, 0): 4}
    step_at = {(1, 0, 0): 0, (1, 0, 1): 1, (2, 0, 0): 2, (2, 0, 1): 3, (2, 1, 1): 4}

    def over_link(d, g, h):
        at = hop_at[d, h]
        return remote(
            parts_ref.at[d, 0, g, halves[h]], parts_ref.at[d, 1, g, halves[h]],
            hop_send.at[g, at], hop_recv.at[g, at], link_mate,
        )

    def over_core(d, s, g, h):
        at = d * 2 + s
        return remote(
            parts_ref.at[d, s, g, halves[h]], parts_ref.at[d, s + 2, g, halves[h]],
            join_send.at[g, at, h], join_recv.at[g, at, h], core_mate,
        )

    def over_scan(d, s, g, h):
        at = step_at[d, s, h]
        source = own_far.at[g] if d == 1 else parts_ref.at[0, s, g]
        return remote(
            source.at[halves[h]], parts_ref.at[d, s, g, halves[h]],
            step_send.at[g, at], step_recv.at[g, at], after[d - 1],
        )

    def by_columns(high, low, table):
        return three_products(high, low, tables_ref[table], tables_ref[table + 1])

    def transform(g):
        rows = strip_rows * share
        for half in range(2):
            block = (near if half == 0 else far)[g]
            tall = jnp.concatenate(
                [block[:, :share].reshape(rows, window), block[:, share:].reshape(rows, window)], axis=1
            )
            high, low = split_two(tall)
            done = by_columns(high, low, 0)
            for c in range(2):
                waves[c, half * rows : (half + 1) * rows, :] = done[:, c * window : (c + 1) * window]

        for p in range(0, share, 2):
            columns = []
            for k in range(2):
                columns.append(
                    jnp.concatenate(
                        [waves[c, pl.ds(p + k, window, stride=share), :] for c in range(2)], axis=0
                    )
                )
            high, low = split_two(jnp.concatenate(columns, axis=1))
            wave = three_products(tables_ref[4], tables_ref[5], high, low)
            wave_re, wave_im = wave[:window], wave[window:]
            at = g * share + p
            values = jnp.concatenate([measured[at], measured[at + 1]], axis=1)
            modulus = jnp.sqrt(wave_re * wave_re + wave_im * wave_im + ETA)
            keep_share = 1.0 - values / modulus
            high, low = split_two(jnp.concatenate([wave_re * keep_share, wave_im * keep_share], axis=0))
            back = three_products(tables_ref[6], tables_ref[7], high, low)
            for k in range(2):
                for c in range(2):
                    backs[c, pl.ds(p + k, window, stride=share), :] = back[
                        c * window : (c + 1) * window, k * window : (k + 1) * window
                    ]

        live = live_ref[g * share : (g + 1) * share][None]
        for half in (1, 0):
            tall = jnp.concatenate(
                [backs[c, half * rows : (half + 1) * rows, :] for c in range(2)], axis=1
            )
            high, low = split_two(tall)
            done = by_columns(high, low, 2)
            pieces = [
                done[:, c * window : (c + 1) * window].reshape(strip_rows, share, window) * live
                for c in range(2)
            ]
            value = jnp.concatenate(pieces, axis=1).astype(BF16)
            if half:
                own_far[g] = value
                for h in range(2):
                    over_scan(1, 0, g, h).start()
            else:
                parts_ref[0, 0, g] = value
                for h in (1, 0):
                    over_link(0, g, h).start()
                for h in range(2):
                    over_scan(2, 0, g, h).start()
                    over_core(0, 0, g, h).start()

    def got_scan(d, s, g, h, link):
        over_scan(d, s, g, h).wait_recv()
        if link:
            over_link(d, g, h).start()
        over_core(d, s, g, h).start()

    def got_link(d, g, h, scan):
        over_link(d, g, h).wait_recv()
        if scan:
            over_scan(2, 1, g, h).start()
        over_core(d, 1, g, h).start()

    def relay(g):
        got_scan(1, 0, g, 0, True)
        got_scan(1, 0, g, 1, True)
        got_link(0, g, 1, True)
        got_link(0, g, 0, False)
        got_scan(2, 0, g, 0, True)
        got_scan(2, 0, g, 1, False)
        got_link(1, g, 0, False)
        got_link(1, g, 1, False)
        got_scan(2, 1, g, 1, False)
        got_link(2, g, 0, False)

    early = range(chunks // 2)
    for chunk in range(chunks):
        compute(chunk)
        if chunk:
            after_core(0, chunk - 1)
    after_core(0, chunks - 1)
    for chunk in early:
        after_zed(0, chunk)
    for chunk in range(chunks):
        after_core(1, chunk)
    for at in range(0, matrix_ref.shape[0], window):
        turned_ref[:, at : at + window] = matrix_ref[at : at + window, :].astype(F32).T.astype(BF16)
    for chunk in range(chunks):
        after_link(0, chunk)
    for chunk in early:
        after_zed(1, chunk)
    for chunk in range(chunks):
        finish(0, chunk)
    side_loads[2].wait()
    side_loads[3].wait()
    transform(0)
    for chunk in range(chunks):
        after_link(1, chunk)
    for chunk in range(chunks):
        finish(1, chunk)
    transform(1)
    for g in range(groups):
        relay(g)

    for chunk in range(chunks):
        to_core(chunk).wait_send()
        for g in range(groups):
            to_link(g, chunk, 0).wait_send()
            to_scan(g, chunk, 0).wait_send()
            if chunk < chunks // 2:
                to_link(g, chunk, 1).wait_send()
                to_zed(g, chunk).wait_send()
            else:
                to_scan(g, chunk, 1).wait_send()
    for g in range(groups):
        for d in range(3):
            for s in range(2):
                for h in range(2):
                    over_core(d, s, g, h).wait()
        for d, h in hop_at:
            over_link(d, g, h).wait_send()
        for d, s, h in step_at:
            over_scan(d, s, g, h).wait_send()


def waves_to_gradients(spots, freq, amp, live, tables, strip, amplitude, shares, scan_size,
                       groups=2, block_rows=8):
    _, beams, strip_rows, window = strip.shape
    per_tile = spots.shape[1]
    share_rows = per_tile // shares
    group = 2 * share_rows
    depth = group // groups
    field_rows = strip_rows * scan_size
    chunks = strip_rows // block_rows
    pairs = shares // 2
    assert groups == 2 and shares == 4 and scan_size > 4 and chunks % 2 == 0
    assert field_rows & (field_rows - 1) == 0 and window & (window - 1) == 0
    tail = (block_rows, depth, window)
    vmem = pl.BlockSpec(memory_space=pltpu.VMEM)
    hbm = pl.BlockSpec(memory_space=pltpu.HBM)
    dma = pltpu.SemaphoreType.DMA
    stays = [
        pltpu.with_memory_space_constraint(v, pltpu.HBM) for v in (freq, amp, tables, strip, amplitude)
    ]
    return pl.pallas_call(
        functools.partial(wave_kernel, shares, scan_size),
        out_shape=[
            jax.ShapeDtypeStruct((3, shares, groups, strip_rows, depth, window), BF16),
            jax.ShapeDtypeStruct((2 * beams, 3 * shares * group), BF16),
            jax.ShapeDtypeStruct((2, shares * group, window), jnp.int32),
        ],
        in_specs=[vmem] * 2 + [hbm] * 5,
        out_specs=[vmem] * 3,
        scratch_shapes=[
            pltpu.VMEM((3 * shares * group, 2 * beams), BF16),
            pltpu.VMEM(freq.shape, jnp.int32),
            pltpu.VMEM(amp.shape, F32),
            pltpu.VMEM(tables.shape, BF16),
            pltpu.VMEM((2, 2, per_tile, window), jnp.int32),
            pltpu.VMEM((2, 2, beams, block_rows, window), BF16),
            pltpu.VMEM((2 * beams * block_rows, window), F32),
            pltpu.VMEM((chunks, pairs, 3, block_rows, group, window), F32),
            pltpu.VMEM((chunks, pairs, 3, block_rows, group, window), BF16),
            pltpu.VMEM((chunks, pairs, 3, block_rows, group, window), BF16),
            pltpu.VMEM((groups, chunks, 3) + tail, BF16),
            pltpu.VMEM((groups, chunks, 3) + tail, BF16),
            pltpu.VMEM((groups, chunks // 2, 2) + tail, BF16),
            pltpu.VMEM((groups, chunks // 2, 2) + tail, BF16),
            pltpu.VMEM((groups, chunks, 2) + tail, BF16),
            pltpu.VMEM((groups, chunks, 2) + tail, BF16),
            pltpu.VMEM((groups, strip_rows, depth, window), F32),
            pltpu.VMEM((groups, strip_rows, depth, window), F32),
            pltpu.VMEM((share_rows, window, window), F32),
            pltpu.VMEM((2, window * share_rows // groups, window), F32),
            pltpu.VMEM((2, window * share_rows // groups, window), F32),
            pltpu.VMEM((groups, strip_rows, depth, window), BF16),
            dma((2,)),
            dma((4,)),
            dma((2,)),
            dma((2,)),
            dma((chunks,)),
            dma((chunks,)),
            dma((groups, chunks, 2)),
            dma((groups, chunks, 2)),
            dma((groups, chunks // 2)),
            dma((groups, chunks // 2)),
            dma((groups, chunks, 2)),
            dma((groups, chunks, 2)),
            dma((groups, 5)),
            dma((groups, 5)),
            dma((groups, 5)),
            dma((groups, 5)),
            dma((groups, 6, 2)),
            dma((groups, 6, 2)),
        ],
        compiler_params=pltpu.CompilerParams(
            collective_id=0, has_side_effects=True, vmem_limit_bytes=40 << 20
        ),
        cost_estimate=pl.CostEstimate(
            flops=12 * per_tile * beams * strip_rows * window,
            bytes_accessed=4 * beams * strip_rows * window,
            transcendentals=0,
        ),
    )(spots, live, *stays)


def backward_kernel(block_rows, offset_ref, matrix_ref, parts_ref, out_ref, wide):
    depth = matrix_ref.shape[0]
    window = out_ref.shape[3]
    first = pl.program_id(0) * block_rows
    kinds, shares, groups = parts_ref.shape[:3]
    for row in range(0, block_rows, 2):
        sides = []
        for k in range(2):
            here = first + row + k
            strips = []
            for d in range(kinds):
                tall = jnp.concatenate(
                    [parts_ref[d, s, g, row + k] for s in range(shares) for g in range(groups)], axis=0
                )
                if d == 0:
                    tall = jnp.where(here >= offset_ref[0], tall.astype(F32), 0.0).astype(BF16)
                if d == 2:
                    tall = jnp.where(here < offset_ref[1], tall.astype(F32), 0.0).astype(BF16)
                strips.append(tall)
            sides.append(jnp.concatenate(strips, axis=0))
        sums = jnp.dot(
            matrix_ref[...], jnp.concatenate(sides, axis=1), preferred_element_type=F32
        )
        for k in range(2):
            wide[pl.ds(row + k, depth, stride=block_rows), :] = sums[:, k * window : (k + 1) * window]
    out_ref[...] = wide[...].reshape(out_ref.shape).astype(BF16)


def backward(matrix, offsets, parts, beams, block_rows=8):
    kinds, shares, groups, strip_rows, depth, window = parts.shape
    return pl.pallas_call(
        functools.partial(backward_kernel, block_rows),
        grid=(strip_rows // block_rows,),
        out_shape=jax.ShapeDtypeStruct((2, beams, strip_rows, window), BF16),
        in_specs=[
            pl.BlockSpec(offsets.shape, lambda i: (0, 0, 0)),
            pl.BlockSpec(matrix.shape, lambda i: (0, 0)),
            pl.BlockSpec(
                (kinds, shares, groups, block_rows, depth, window), lambda i: (0, 0, 0, i, 0, 0)
            ),
        ],
        out_specs=pl.BlockSpec((2, beams, block_rows, window), lambda i: (0, 0, i, 0)),
        scratch_shapes=[pltpu.VMEM((2 * beams * block_rows, window), F32)],
        compiler_params=pltpu.CompilerParams(vmem_limit_bytes=28 << 20),
        cost_estimate=pl.CostEstimate(
            flops=2 * matrix.size * strip_rows * window,
            bytes_accessed=4 * beams * strip_rows * window + 2 * parts.size,
            transcendentals=0,
        ),
    )(offsets, matrix, parts)


def transform_tables(window):
    counter = np.arange(window)
    turn_angle = (counter[:, None] * counter[None, :] % window) * (2.0 * np.pi / window)
    table_re = np.cos(turn_angle) / np.sqrt(window)
    table_im = -np.sin(turn_angle) / np.sqrt(window)
    stacked = []
    for left in (False, True):
        for sign in (1.0, -1.0):
            imag = sign * table_im
            if left:
                full = np.block([[table_re, -imag], [imag, table_re]])
            else:
                full = np.block([[table_re, imag], [-imag, table_re]])
            high = full.astype(BF16)
            stacked += [high, (full - high.astype(np.float64)).astype(BF16)]
    return jnp.asarray(np.stack(stacked))


def body(smatrix, beam_freq, beam_amp, row_offset, col_offset, counts, amplitude):
    beam_dev = smatrix.shape[1]
    window = smatrix.shape[3]
    per_tile = row_offset.shape[0]
    scan_size = lax.axis_size("scan")
    shares = lax.axis_size("beam")
    share_rows = per_tile // shares
    assert window == 2 * smatrix.shape[2]
    spots = jnp.broadcast_to(
        jnp.stack([row_offset, col_offset])[:, :, None], (2, per_tile, window)
    )
    first_row = lax.axis_index("beam") * share_rows
    live = (first_row + jnp.arange(share_rows, dtype=jnp.int32) < counts[0]).astype(F32)
    live = jnp.broadcast_to(live[:, None], (share_rows, window))
    parts, matrix, offsets = waves_to_gradients(
        spots, beam_freq, beam_amp, live, transform_tables(window), smatrix, amplitude, shares, scan_size
    )
    return backward(matrix, offsets, parts, beam_dev)


def solution(mesh):
    return jax.shard_map(
        body,
        mesh=mesh,
        in_specs=(
            P(None, "beam", "scan", None),
            P(None, "beam"),
            P(None, "beam"),
            P("scan"),
            P("scan"),
            P("scan"),
            P("scan", None, None),
        ),
        out_specs=P(None, "beam", "scan", None),
        check_vma=False,
    )
```

```python
import functools

import jax
import jax.numpy as jnp
import numpy as np
from jax import lax
from jax.experimental import pallas as pl
from jax.experimental.pallas import tpu as pltpu
from jax.sharding import PartitionSpec as P

TWO_PI = 6.283185307179586
ETA = 0.1
F32 = jnp.float32
BF16 = jnp.bfloat16
MESH = pl.DeviceIdType.MESH


def split_two(value):
    high = value.astype(BF16)
    return high, (value - high.astype(F32)).astype(BF16)


def three_products(left_high, left_low, right_high, right_low):
    total = jnp.dot(left_low, right_high, preferred_element_type=F32)
    total += jnp.dot(left_high, right_low, preferred_element_type=F32)
    return total + jnp.dot(left_high, right_high, preferred_element_type=F32)


def wave_kernel(shares, scan_size, spots_ref, live_ref, freq_hbm, amp_hbm, tables_hbm, strip_ref,
                amplitude_ref, parts_ref, turned_ref, offset_ref,
                matrix_ref, freq_ref, amp_ref, tables_ref, spots, spread, strips, wide, kept, core_out, core_in, link_out, link_in, zed_out, zed_in,
                scan_out, scan_in, near, far, measured, waves, backs, own_far,
                load_sem, side_sem, spot_send, spot_recv, pair_send, pair_recv, link_send, link_recv,
                zed_send, zed_recv, scan_send, scan_recv,
                hop_send, hop_recv, step_send, step_recv, join_send, join_recv):
    chunks, pairs, _, block_rows, group, window = kept.shape
    _, _, groups, strip_rows, depth, _ = parts_ref.shape
    beams = strip_ref.shape[1]
    share = depth // 2
    share_rows = group // 2
    field_rows = strip_rows * scan_size
    me = lax.axis_index("beam")
    tile = lax.axis_index("scan")
    core_id = me + 1 - 2 * lax.rem(me, 2)
    core_mate = {"beam": core_id}
    link_mate = {"beam": lax.rem(me + pairs, shares)}
    share_ids = [me, lax.rem(me + pairs, shares), core_id, lax.rem(core_id + pairs, shares)]
    before = [{"scan": lax.rem(tile + scan_size - d, scan_size)} for d in (1, 2)]
    after = [{"scan": lax.rem(tile + d, scan_size)} for d in (1, 2)]

    def load(chunk):
        return pltpu.make_async_copy(
            strip_ref.at[:, :, pl.ds(chunk * block_rows, block_rows), :],
            strips.at[chunk % 2],
            load_sem.at[chunk % 2],
        )

    def remote(source, target, sends, recvs, device):
        return pltpu.make_async_remote_copy(
            source, target, sends, recvs, device_id=device, device_id_type=MESH
        )

    def spot_copy(d):
        return remote(spots_ref, spots.at[d - 1], spot_send.at[d - 1], spot_recv.at[d - 1], after[d - 1])

    side_loads = [
        pltpu.make_async_copy(source, target, side_sem.at[i])
        for i, (source, target) in enumerate(
            [
                (freq_hbm, freq_ref),
                (amp_hbm, amp_ref),
                (tables_hbm, tables_ref),
                (amplitude_ref.at[pl.ds(me * share_rows, share_rows)], measured),
            ]
        )
    ]
    side_loads[0].start()
    side_loads[1].start()
    load(0).start()
    load(1).start()
    side_loads[2].start()
    side_loads[3].start()
    barrier = pltpu.get_barrier_semaphore()
    peers = [core_mate, link_mate] + before + after
    for peer in peers:
        pl.semaphore_signal(barrier, inc=1, device_id=peer, device_id_type=MESH)
    pl.semaphore_wait(barrier, len(peers))
    spot_copy(1).start()
    spot_copy(2).start()

    def coefficients(d):
        source = spots_ref if d == 0 else spots.at[d - 1]
        for c in range(2):
            line = jnp.broadcast_to(source[c : c + 1, :].astype(F32), (window, window))
            spread[c] = line.T.astype(jnp.int32)
        tile_id = lax.rem(tile + scan_size - d, scan_size)
        for s in range(shares):
            here = pl.ds(share_ids[s] * share_rows, share_rows)
            rows = spread[0, here, :]
            cols = spread[1, here, :]
            base = (d * shares + s) * group
            if d != 1:
                at = s * group
                for g in range(groups):
                    own = rows[g * share : (g + 1) * share]
                    offset_ref[d // 2, at + g * depth : at + (g + 1) * depth, :] = jnp.concatenate(
                        [own, own], axis=0
                    )
            for lane in range(0, beams, window):
                lanes = slice(lane, lane + window)
                along_rows = (freq_ref[0:1, lanes] * (tile_id * strip_rows + rows)) & (field_rows - 1)
                along_cols = (freq_ref[1:2, lanes] * cols) & (window - 1)
                turns = along_rows.astype(F32) / field_rows + along_cols.astype(F32) / window
                angle = -TWO_PI * turns
                cos_part = jnp.cos(angle)
                sin_part = jnp.sin(angle)
                coef_re = amp_ref[0:1, lanes] * cos_part - amp_ref[1:2, lanes] * sin_part
                coef_im = amp_ref[0:1, lanes] * sin_part + amp_ref[1:2, lanes] * cos_part
                for g in range(groups):
                    re = coef_re[g * share : (g + 1) * share]
                    im = coef_im[g * share : (g + 1) * share]
                    spot = slice(base + g * depth, base + (g + 1) * depth)
                    matrix_ref[spot, lanes] = jnp.concatenate([re, im], axis=0).astype(BF16)
                    matrix_ref[spot, beams + lane : beams + lane + window] = jnp.concatenate(
                        [-im, re], axis=0
                    ).astype(BF16)

    side_loads[0].wait()
    side_loads[1].wait()
    coefficients(0)
    for d in (1, 2):
        spot_copy(d).wait()
        coefficients(d)

    def to_core(chunk):
        return remote(
            core_out.at[chunk], core_in.at[chunk], pair_send.at[chunk], pair_recv.at[chunk], core_mate
        )

    def to_link(g, chunk, late):
        if chunk >= chunks // 2:
            pieces = slice(0, 3)
        elif late:
            pieces = slice(0, 1)
        else:
            pieces = slice(1, 2)
        pieces = pl.ds(pieces.start, pieces.stop - pieces.start)
        return remote(
            link_out.at[g, chunk, pieces], link_in.at[g, chunk, pieces],
            link_send.at[g, chunk, late], link_recv.at[g, chunk, late], link_mate,
        )

    def to_zed(g, chunk):
        return remote(
            zed_out.at[g, chunk], zed_in.at[g, chunk],
            zed_send.at[g, chunk], zed_recv.at[g, chunk], before[1],
        )

    def to_scan(g, chunk, which):
        return remote(
            scan_out.at[g, chunk, which], scan_in.at[g, chunk, which],
            scan_send.at[g, chunk, which], scan_recv.at[g, chunk, which], before[which],
        )

    def compute(chunk):
        load(chunk).wait()
        wide[...] = strips[chunk % 2].astype(F32).reshape(2 * beams * block_rows, window)
        if chunk + 2 < chunks:
            load(chunk + 2).start()

        def pair_of_rows(step, carry):
            row = step * 2
            rhs = jnp.concatenate(
                [wide[pl.ds(row + k, 2 * beams, stride=block_rows), :] for k in range(2)], axis=1
            ).astype(BF16)
            sums = jnp.dot(matrix_ref[...], rhs, preferred_element_type=F32)
            for k in range(2):
                here = chunk * block_rows + row + k
                for d in range(3):
                    for s in range(shares):
                        at = (d * shares + s) * group
                        piece = sums[at : at + group, k * window : (k + 1) * window]
                        if d == 0:
                            piece = jnp.where(here >= offset_ref[0, s * group : (s + 1) * group], piece, 0.0)
                        if d == 2:
                            piece = jnp.where(here < offset_ref[1, s * group : (s + 1) * group], piece, 0.0)
                        if s < pairs:
                            kept[chunk, s, d, row + k] = piece
                        else:
                            core_out[chunk, s - pairs, d, row + k] = piece.astype(BF16)
            return carry

        lax.fori_loop(0, block_rows // 2, pair_of_rows, 0)
        to_core(chunk).start()

    def held(g, chunk, s, d):
        part = slice(g * depth, (g + 1) * depth)
        return kept[chunk, s, d, :, part, :] + core_in[chunk, s, d, :, part, :].astype(F32)

    def after_core(g, chunk):
        if g == 0:
            to_core(chunk).wait_recv()
        link_out[g, chunk, 1] = held(g, chunk, 1, 1).astype(BF16)
        if chunk < chunks // 2:
            for s in range(2):
                zed_out[g, chunk, s] = held(g, chunk, s, 2).astype(BF16)
            to_zed(g, chunk).start()
        else:
            for d in (0, 2):
                link_out[g, chunk, d] = held(g, chunk, 1, d).astype(BF16)
        to_link(g, chunk, 0).start()

    def after_zed(g, chunk):
        to_zed(g, chunk).wait_recv()
        link_out[g, chunk, 0] = (held(g, chunk, 1, 0) + zed_in[g, chunk, 1].astype(F32)).astype(BF16)
        to_link(g, chunk, 1).start()

    def rows_of(chunk):
        return slice(chunk * block_rows, (chunk + 1) * block_rows)

    def after_link(g, chunk):
        to_link(g, chunk, 0).wait_recv()
        for d in (1, 2) if chunk >= chunks // 2 else (1,):
            scan_out[g, chunk, d - 1] = (
                held(g, chunk, 0, d) + link_in[g, chunk, d].astype(F32)
            ).astype(BF16)
            to_scan(g, chunk, d - 1).start()
        if chunk >= chunks // 2:
            near[g, rows_of(chunk)] = held(g, chunk, 0, 0) + link_in[g, chunk, 0].astype(F32)

    def finish(g, chunk):
        if chunk < chunks // 2:
            to_link(g, chunk, 1).wait_recv()
            near[g, rows_of(chunk)] = (
                held(g, chunk, 0, 0)
                + zed_in[g, chunk, 0].astype(F32)
                + link_in[g, chunk, 0].astype(F32)
            )
        to_scan(g, chunk, 0).wait_recv()
        far[g, rows_of(chunk)] = scan_in[g, chunk, 0].astype(F32)
        if chunk >= chunks // 2:
            to_scan(g, chunk, 1).wait_recv()
            near[g, rows_of(chunk)] += scan_in[g, chunk, 1].astype(F32)

    half_rows = strip_rows // 2
    halves = [pl.ds(h * half_rows, half_rows) for h in range(2)]
    hop_at = {(0, 0): 0, (0, 1): 1, (1, 0): 2, (1, 1): 3, (2, 0): 4}
    step_at = {(1, 0, 0): 0, (1, 0, 1): 1, (2, 0, 0): 2, (2, 0, 1): 3, (2, 1, 1): 4}

    def over_link(d, g, h):
        at = hop_at[d, h]
        return remote(
            parts_ref.at[d, 0, g, halves[h]], parts_ref.at[d, 1, g, halves[h]],
            hop_send.at[g, at], hop_recv.at[g, at], link_mate,
        )

    def over_core(d, s, g, h):
        at = d * 2 + s
        return remote(
            parts_ref.at[d, s, g, halves[h]], parts_ref.at[d, s + 2, g, halves[h]],
            join_send.at[g, at, h], join_recv.at[g, at, h], core_mate,
        )

    def over_scan(d, s, g, h):
        at = step_at[d, s, h]
        source = own_far.at[g] if d == 1 else parts_ref.at[0, s, g]
        return remote(
            source.at[halves[h]], parts_ref.at[d, s, g, halves[h]],
            step_send.at[g, at], step_recv.at[g, at], after[d - 1],
        )

    def by_columns(high, low, table):
        return three_products(high, low, tables_ref[table], tables_ref[table + 1])

    def transform(g):
        rows = strip_rows * share
        for half in range(2):
            block = (near if half == 0 else far)[g]
            tall = jnp.concatenate(
                [block[:, :share].reshape(rows, window), block[:, share:].reshape(rows, window)], axis=1
            )
            high, low = split_two(tall)
            done = by_columns(high, low, 0)
            for c in range(2):
                waves[c, half * rows : (half + 1) * rows, :] = done[:, c * window : (c + 1) * window]

        for p in range(0, share, 2):
            columns = []
            for k in range(2):
                columns.append(
                    jnp.concatenate(
                        [waves[c, pl.ds(p + k, window, stride=share), :] for c in range(2)], axis=0
                    )
                )
            high, low = split_two(jnp.concatenate(columns, axis=1))
            wave = three_products(tables_ref[4], tables_ref[5], high, low)
            wave_re, wave_im = wave[:window], wave[window:]
            at = g * share + p
            values = jnp.concatenate([measured[at], measured[at + 1]], axis=1)
            modulus = jnp.sqrt(wave_re * wave_re + wave_im * wave_im + ETA)
            keep_share = 1.0 - values / modulus
            high, low = split_two(jnp.concatenate([wave_re * keep_share, wave_im * keep_share], axis=0))
            back = three_products(tables_ref[6], tables_ref[7], high, low)
            for k in range(2):
                for c in range(2):
                    backs[c, pl.ds(p + k, window, stride=share), :] = back[
                        c * window : (c + 1) * window, k * window : (k + 1) * window
                    ]

        live = live_ref[g * share : (g + 1) * share][None]
        for half in (1, 0):
            tall = jnp.concatenate(
                [backs[c, half * rows : (half + 1) * rows, :] for c in range(2)], axis=1
            )
            high, low = split_two(tall)
            done = by_columns(high, low, 2)
            pieces = [
                done[:, c * window : (c + 1) * window].reshape(strip_rows, share, window) * live
                for c in range(2)
            ]
            value = jnp.concatenate(pieces, axis=1).astype(BF16)
            if half:
                own_far[g] = value
                for h in range(2):
                    over_scan(1, 0, g, h).start()
            else:
                parts_ref[0, 0, g] = value
                for h in (1, 0):
                    over_link(0, g, h).start()
                for h in range(2):
                    over_scan(2, 0, g, h).start()
                    over_core(0, 0, g, h).start()

    def got_scan(d, s, g, h, link):
        over_scan(d, s, g, h).wait_recv()
        if link:
            over_link(d, g, h).start()
        over_core(d, s, g, h).start()

    def got_link(d, g, h, scan):
        over_link(d, g, h).wait_recv()
        if scan:
            over_scan(2, 1, g, h).start()
        over_core(d, 1, g, h).start()

    def relay(g):
        got_scan(1, 0, g, 0, True)
        got_scan(1, 0, g, 1, True)
        got_link(0, g, 1, True)
        got_link(0, g, 0, False)
        got_scan(2, 0, g, 0, True)
        got_scan(2, 0, g, 1, False)
        got_link(1, g, 0, False)
        got_link(1, g, 1, False)
        got_scan(2, 1, g, 1, False)
        got_link(2, g, 0, False)

    early = range(chunks // 2)
    for chunk in range(chunks):
        compute(chunk)
        if chunk:
            after_core(0, chunk - 1)
            if chunk - 1 in early:
                after_core(1, chunk - 1)
    after_core(0, chunks - 1)
    for chunk in early:
        after_zed(0, chunk)
    for chunk in range(chunks // 2, chunks):
        after_core(1, chunk)
    for at in range(0, matrix_ref.shape[0], window):
        turned_ref[:, at : at + window] = matrix_ref[at : at + window, :].astype(F32).T.astype(BF16)
    for chunk in early:
        after_link(0, chunk)
        after_zed(1, chunk)
    for chunk in range(chunks // 2, chunks):
        after_link(0, chunk)
    for chunk in early:
        after_link(1, chunk)
    for chunk in range(chunks):
        finish(0, chunk)
    side_loads[2].wait()
    side_loads[3].wait()
    transform(0)
    for chunk in range(chunks // 2, chunks):
        after_link(1, chunk)
    for chunk in range(chunks):
        finish(1, chunk)
    transform(1)
    for g in range(groups):
        relay(g)

    for chunk in range(chunks):
        to_core(chunk).wait_send()
        for g in range(groups):
            to_link(g, chunk, 0).wait_send()
            to_scan(g, chunk, 0).wait_send()
            if chunk < chunks // 2:
                to_link(g, chunk, 1).wait_send()
                to_zed(g, chunk).wait_send()
            else:
                to_scan(g, chunk, 1).wait_send()
    for g in range(groups):
        for d in range(3):
            for s in range(2):
                for h in range(2):
                    over_core(d, s, g, h).wait()
        for d, h in hop_at:
            over_link(d, g, h).wait_send()
        for d, s, h in step_at:
            over_scan(d, s, g, h).wait_send()


def waves_to_gradients(per_tile, spots, freq, amp, live, tables, strip, amplitude, shares, scan_size,
                       groups=2, block_rows=8):
    _, beams, strip_rows, window = strip.shape
    share_rows = per_tile // shares
    group = 2 * share_rows
    depth = group // groups
    field_rows = strip_rows * scan_size
    chunks = strip_rows // block_rows
    pairs = shares // 2
    assert groups == 2 and shares == 4 and scan_size > 4 and chunks % 2 == 0
    assert field_rows & (field_rows - 1) == 0 and window & (window - 1) == 0
    tail = (block_rows, depth, window)
    vmem = pl.BlockSpec(memory_space=pltpu.VMEM)
    hbm = pl.BlockSpec(memory_space=pltpu.HBM)
    dma = pltpu.SemaphoreType.DMA
    stays = [
        pltpu.with_memory_space_constraint(v, pltpu.HBM) for v in (freq, amp, tables, strip, amplitude)
    ]
    return pl.pallas_call(
        functools.partial(wave_kernel, shares, scan_size),
        out_shape=[
            jax.ShapeDtypeStruct((3, shares, groups, strip_rows, depth, window), BF16),
            jax.ShapeDtypeStruct((2 * beams, 3 * shares * group), BF16),
            jax.ShapeDtypeStruct((2, shares * group, window), jnp.int32),
        ],
        in_specs=[vmem] * 2 + [hbm] * 5,
        out_specs=[vmem] * 3,
        scratch_shapes=[
            pltpu.VMEM((3 * shares * group, 2 * beams), BF16),
            pltpu.VMEM(freq.shape, jnp.int32),
            pltpu.VMEM(amp.shape, F32),
            pltpu.VMEM(tables.shape, BF16),
            pltpu.VMEM((2,) + spots.shape, jnp.int32),
            pltpu.VMEM((2, window, window), jnp.int32),
            pltpu.VMEM((2, 2, beams, block_rows, window), BF16),
            pltpu.VMEM((2 * beams * block_rows, window), F32),
            pltpu.VMEM((chunks, pairs, 3, block_rows, group, window), F32),
            pltpu.VMEM((chunks, pairs, 3, block_rows, group, window), BF16),
            pltpu.VMEM((chunks, pairs, 3, block_rows, group, window), BF16),
            pltpu.VMEM((groups, chunks, 3) + tail, BF16),
            pltpu.VMEM((groups, chunks, 3) + tail, BF16),
            pltpu.VMEM((groups, chunks // 2, 2) + tail, BF16),
            pltpu.VMEM((groups, chunks // 2, 2) + tail, BF16),
            pltpu.VMEM((groups, chunks, 2) + tail, BF16),
            pltpu.VMEM((groups, chunks, 2) + tail, BF16),
            pltpu.VMEM((groups, strip_rows, depth, window), F32),
            pltpu.VMEM((groups, strip_rows, depth, window), F32),
            pltpu.VMEM((share_rows, window, window), F32),
            pltpu.VMEM((2, window * share_rows // groups, window), F32),
            pltpu.VMEM((2, window * share_rows // groups, window), F32),
            pltpu.VMEM((groups, strip_rows, depth, window), BF16),
            dma((2,)),
            dma((4,)),
            dma((2,)),
            dma((2,)),
            dma((chunks,)),
            dma((chunks,)),
            dma((groups, chunks, 2)),
            dma((groups, chunks, 2)),
            dma((groups, chunks // 2)),
            dma((groups, chunks // 2)),
            dma((groups, chunks, 2)),
            dma((groups, chunks, 2)),
            dma((groups, 5)),
            dma((groups, 5)),
            dma((groups, 5)),
            dma((groups, 5)),
            dma((groups, 6, 2)),
            dma((groups, 6, 2)),
        ],
        compiler_params=pltpu.CompilerParams(
            collective_id=0, has_side_effects=True, vmem_limit_bytes=40 << 20
        ),
        cost_estimate=pl.CostEstimate(
            flops=12 * per_tile * beams * strip_rows * window,
            bytes_accessed=4 * beams * strip_rows * window,
            transcendentals=0,
        ),
    )(spots, live, *stays)


def backward_kernel(block_rows, offset_ref, matrix_ref, parts_ref, out_ref, wide):
    depth = matrix_ref.shape[0]
    window = out_ref.shape[3]
    first = pl.program_id(0) * block_rows
    kinds, shares, groups = parts_ref.shape[:3]
    for row in range(0, block_rows, 2):
        sides = []
        for k in range(2):
            here = first + row + k
            strips = []
            for d in range(kinds):
                tall = jnp.concatenate(
                    [parts_ref[d, s, g, row + k] for s in range(shares) for g in range(groups)], axis=0
                )
                if d == 0:
                    tall = jnp.where(here >= offset_ref[0], tall.astype(F32), 0.0).astype(BF16)
                if d == 2:
                    tall = jnp.where(here < offset_ref[1], tall.astype(F32), 0.0).astype(BF16)
                strips.append(tall)
            sides.append(jnp.concatenate(strips, axis=0))
        sums = jnp.dot(
            matrix_ref[...], jnp.concatenate(sides, axis=1), preferred_element_type=F32
        )
        for k in range(2):
            wide[pl.ds(row + k, depth, stride=block_rows), :] = sums[:, k * window : (k + 1) * window]
    out_ref[...] = wide[...].reshape(out_ref.shape).astype(BF16)


def backward(matrix, offsets, parts, beams, block_rows=8):
    kinds, shares, groups, strip_rows, depth, window = parts.shape
    return pl.pallas_call(
        functools.partial(backward_kernel, block_rows),
        grid=(strip_rows // block_rows,),
        out_shape=jax.ShapeDtypeStruct((2, beams, strip_rows, window), BF16),
        in_specs=[
            pl.BlockSpec(offsets.shape, lambda i: (0, 0, 0)),
            pl.BlockSpec(matrix.shape, lambda i: (0, 0)),
            pl.BlockSpec(
                (kinds, shares, groups, block_rows, depth, window), lambda i: (0, 0, 0, i, 0, 0)
            ),
        ],
        out_specs=pl.BlockSpec((2, beams, block_rows, window), lambda i: (0, 0, i, 0)),
        scratch_shapes=[pltpu.VMEM((2 * beams * block_rows, window), F32)],
        compiler_params=pltpu.CompilerParams(vmem_limit_bytes=28 << 20),
        cost_estimate=pl.CostEstimate(
            flops=2 * matrix.size * strip_rows * window,
            bytes_accessed=4 * beams * strip_rows * window + 2 * parts.size,
            transcendentals=0,
        ),
    )(offsets, matrix, parts)


def transform_tables(window):
    counter = np.arange(window)
    turn_angle = (counter[:, None] * counter[None, :] % window) * (2.0 * np.pi / window)
    table_re = np.cos(turn_angle) / np.sqrt(window)
    table_im = -np.sin(turn_angle) / np.sqrt(window)
    stacked = []
    for left in (False, True):
        for sign in (1.0, -1.0):
            imag = sign * table_im
            if left:
                full = np.block([[table_re, -imag], [imag, table_re]])
            else:
                full = np.block([[table_re, imag], [-imag, table_re]])
            high = full.astype(BF16)
            stacked += [high, (full - high.astype(np.float64)).astype(BF16)]
    return jnp.asarray(np.stack(stacked))


def body(smatrix, beam_freq, beam_amp, row_offset, col_offset, counts, amplitude):
    beam_dev = smatrix.shape[1]
    window = smatrix.shape[3]
    per_tile = row_offset.shape[0]
    scan_size = lax.axis_size("scan")
    shares = lax.axis_size("beam")
    share_rows = per_tile // shares
    assert window == 2 * smatrix.shape[2]
    assert per_tile <= window
    spots = jnp.pad(jnp.stack([row_offset, col_offset]), ((0, 6), (0, window - per_tile)))
    first_row = lax.axis_index("beam") * share_rows
    live = (first_row + jnp.arange(share_rows, dtype=jnp.int32) < counts[0]).astype(F32)
    live = jnp.broadcast_to(live[:, None], (share_rows, window))
    parts, matrix, offsets = waves_to_gradients(
        per_tile, spots, beam_freq, beam_amp, live, transform_tables(window), smatrix, amplitude, shares, scan_size
    )
    return backward(matrix, offsets, parts, beam_dev)


def solution(mesh):
    return jax.shard_map(
        body,
        mesh=mesh,
        in_specs=(
            P(None, "beam", "scan", None),
            P(None, "beam"),
            P(None, "beam"),
            P("scan"),
            P("scan"),
            P("scan"),
            P("scan", None, None),
        ),
        out_specs=P(None, "beam", "scan", None),
        check_vma=False,
    )
```

```python
import functools

import jax
import jax.numpy as jnp
import numpy as np
from jax import lax
from jax.experimental import pallas as pl
from jax.experimental.pallas import tpu as pltpu
from jax.sharding import PartitionSpec as P

TWO_PI = 6.283185307179586
ETA = 0.1
F32 = jnp.float32
BF16 = jnp.bfloat16
MESH = pl.DeviceIdType.MESH


def split_two(value):
    high = value.astype(BF16)
    return high, (value - high.astype(F32)).astype(BF16)


def three_products(left_high, left_low, right_high, right_low):
    total = jnp.dot(left_low, right_high, preferred_element_type=F32)
    total += jnp.dot(left_high, right_low, preferred_element_type=F32)
    return total + jnp.dot(left_high, right_high, preferred_element_type=F32)


def wave_kernel(shares, scan_size, spots_ref, live_ref, freq_hbm, amp_hbm, tables_hbm, strip_ref,
                amplitude_ref, parts_ref, turned_ref, offset_ref,
                matrix_ref, freq_ref, amp_ref, tables_ref, spots, spread, strips, wide, kept, core_out, core_in, link_out, link_in, zed_out, zed_in,
                scan_out, scan_in, near, far, measured, waves, backs, own_far,
                load_sem, side_sem, spot_send, spot_recv, pair_send, pair_recv, link_send, link_recv,
                zed_send, zed_recv, scan_send, scan_recv,
                hop_send, hop_recv, step_send, step_recv, join_send, join_recv,
                relay_in, hop_in, relay_send, relay_recv, pass_send, far_send, far_recv, last_send):
    chunks, pairs, _, block_rows, group, window = kept.shape
    _, _, groups, strip_rows, depth, _ = parts_ref.shape
    beams = strip_ref.shape[1]
    share = depth // 2
    share_rows = group // 2
    field_rows = strip_rows * scan_size
    cut = zed_out.shape[1]
    me = lax.axis_index("beam")
    tile = lax.axis_index("scan")
    core_id = me + 1 - 2 * lax.rem(me, 2)
    core_mate = {"beam": core_id}
    link_mate = {"beam": lax.rem(me + pairs, shares)}
    share_ids = [me, lax.rem(me + pairs, shares), core_id, lax.rem(core_id + pairs, shares)]
    before = [{"scan": lax.rem(tile + scan_size - d, scan_size)} for d in (1, 2)]
    after = [{"scan": lax.rem(tile + d, scan_size)} for d in (1, 2)]

    def load(chunk):
        return pltpu.make_async_copy(
            strip_ref.at[:, :, pl.ds(chunk * block_rows, block_rows), :],
            strips.at[chunk % 2],
            load_sem.at[chunk % 2],
        )

    def remote(source, target, sends, recvs, device):
        return pltpu.make_async_remote_copy(
            source, target, sends, recvs, device_id=device, device_id_type=MESH
        )

    def spot_copy(d):
        return remote(spots_ref, spots.at[d - 1], spot_send.at[d - 1], spot_recv.at[d - 1], after[d - 1])

    side_loads = [
        pltpu.make_async_copy(source, target, side_sem.at[i])
        for i, (source, target) in enumerate(
            [
                (freq_hbm, freq_ref),
                (amp_hbm, amp_ref),
                (tables_hbm, tables_ref),
                (amplitude_ref.at[pl.ds(me * share_rows, share_rows)], measured),
            ]
        )
    ]
    side_loads[0].start()
    side_loads[1].start()
    load(0).start()
    load(1).start()
    side_loads[2].start()
    side_loads[3].start()
    barrier = pltpu.get_barrier_semaphore()
    peers = [core_mate, link_mate] + before + after
    for peer in peers:
        pl.semaphore_signal(barrier, inc=1, device_id=peer, device_id_type=MESH)
    pl.semaphore_wait(barrier, len(peers))
    spot_copy(1).start()
    spot_copy(2).start()

    def coefficients(d):
        source = spots_ref if d == 0 else spots.at[d - 1]
        for c in range(2):
            line = jnp.broadcast_to(source[c : c + 1, :].astype(F32), (window, window))
            spread[c] = line.T.astype(jnp.int32)
        tile_id = lax.rem(tile + scan_size - d, scan_size)
        for s in range(shares):
            here = pl.ds(share_ids[s] * share_rows, share_rows)
            rows = spread[0, here, :]
            cols = spread[1, here, :]
            base = (d * shares + s) * group
            if d != 1:
                at = s * group
                for g in range(groups):
                    own = rows[g * share : (g + 1) * share]
                    offset_ref[d // 2, at + g * depth : at + (g + 1) * depth, :] = jnp.concatenate(
                        [own, own], axis=0
                    )
            for lane in range(0, beams, window):
                lanes = slice(lane, lane + window)
                along_rows = (freq_ref[0:1, lanes] * (tile_id * strip_rows + rows)) & (field_rows - 1)
                along_cols = (freq_ref[1:2, lanes] * cols) & (window - 1)
                turns = along_rows.astype(F32) / field_rows + along_cols.astype(F32) / window
                angle = -TWO_PI * turns
                cos_part = jnp.cos(angle)
                sin_part = jnp.sin(angle)
                coef_re = amp_ref[0:1, lanes] * cos_part - amp_ref[1:2, lanes] * sin_part
                coef_im = amp_ref[0:1, lanes] * sin_part + amp_ref[1:2, lanes] * cos_part
                for g in range(groups):
                    re = coef_re[g * share : (g + 1) * share]
                    im = coef_im[g * share : (g + 1) * share]
                    spot = slice(base + g * depth, base + (g + 1) * depth)
                    matrix_ref[spot, lanes] = jnp.concatenate([re, im], axis=0).astype(BF16)
                    matrix_ref[spot, beams + lane : beams + lane + window] = jnp.concatenate(
                        [-im, re], axis=0
                    ).astype(BF16)

    side_loads[0].wait()
    side_loads[1].wait()
    coefficients(0)
    for d in (1, 2):
        spot_copy(d).wait()
        coefficients(d)

    def to_core(chunk):
        return remote(
            core_out.at[chunk], core_in.at[chunk], pair_send.at[chunk], pair_recv.at[chunk], core_mate
        )

    def to_link(g, chunk, late):
        if chunk >= cut:
            pieces = slice(0, 3)
        elif late:
            pieces = slice(0, 1)
        else:
            pieces = slice(1, 2)
        pieces = pl.ds(pieces.start, pieces.stop - pieces.start)
        return remote(
            link_out.at[g, chunk, pieces], link_in.at[g, chunk, pieces],
            link_send.at[g, chunk, late], link_recv.at[g, chunk, late], link_mate,
        )

    def to_zed(g, chunk):
        return remote(
            zed_out.at[g, chunk], zed_in.at[g, chunk],
            zed_send.at[g, chunk], zed_recv.at[g, chunk], before[1],
        )

    def to_scan(g, chunk, which):
        return remote(
            scan_out.at[g, chunk, which], scan_in.at[g, chunk, which],
            scan_send.at[g, chunk, which], scan_recv.at[g, chunk, which], before[which],
        )

    odd = lax.rem(tile, 2) == 1
    even = lax.rem(tile, 2) == 0

    def to_relay(g, chunk):
        at = chunk // 2
        return remote(
            scan_out.at[g, chunk, 0], relay_in.at[g, at],
            relay_send.at[g, at], relay_recv.at[g, at], after[0],
        )

    def from_relay(g, chunk):
        at = chunk // 2
        return remote(
            relay_in.at[g, at], scan_in.at[g, chunk, 0],
            pass_send.at[g, at], scan_recv.at[g, chunk, 0], before[1],
        )

    def pass_on(g, chunk):
        @pl.when(odd)
        def _():
            to_relay(g, chunk).wait_recv()
            from_relay(g, chunk).start()

    def compute(chunk):
        load(chunk).wait()
        wide[...] = strips[chunk % 2].astype(F32).reshape(2 * beams * block_rows, window)
        if chunk + 2 < chunks:
            load(chunk + 2).start()

        def pair_of_rows(step, carry):
            row = step * 2
            rhs = jnp.concatenate(
                [wide[pl.ds(row + k, 2 * beams, stride=block_rows), :] for k in range(2)], axis=1
            ).astype(BF16)
            sums = jnp.dot(matrix_ref[...], rhs, preferred_element_type=F32)
            for k in range(2):
                here = chunk * block_rows + row + k
                for d in range(3):
                    for s in range(shares):
                        at = (d * shares + s) * group
                        piece = sums[at : at + group, k * window : (k + 1) * window]
                        if d == 0:
                            piece = jnp.where(here >= offset_ref[0, s * group : (s + 1) * group], piece, 0.0)
                        if d == 2:
                            piece = jnp.where(here < offset_ref[1, s * group : (s + 1) * group], piece, 0.0)
                        if s < pairs:
                            kept[chunk, s, d, row + k] = piece
                        else:
                            core_out[chunk, s - pairs, d, row + k] = piece.astype(BF16)
            return carry

        lax.fori_loop(0, block_rows // 2, pair_of_rows, 0)
        to_core(chunk).start()

    def held(g, chunk, s, d):
        part = slice(g * depth, (g + 1) * depth)
        return kept[chunk, s, d, :, part, :] + core_in[chunk, s, d, :, part, :].astype(F32)

    def after_core(g, chunk):
        if g == 0:
            to_core(chunk).wait_recv()
        link_out[g, chunk, 1] = held(g, chunk, 1, 1).astype(BF16)
        if chunk < cut:
            for s in range(2):
                zed_out[g, chunk, s] = held(g, chunk, s, 2).astype(BF16)
            to_zed(g, chunk).start()
        else:
            for d in (0, 2):
                link_out[g, chunk, d] = held(g, chunk, 1, d).astype(BF16)
        to_link(g, chunk, 0).start()

    def after_zed(g, chunk):
        to_zed(g, chunk).wait_recv()
        link_out[g, chunk, 0] = (held(g, chunk, 1, 0) + zed_in[g, chunk, 1].astype(F32)).astype(BF16)
        to_link(g, chunk, 1).start()

    def rows_of(chunk):
        return slice(chunk * block_rows, (chunk + 1) * block_rows)

    def after_link(g, chunk):
        to_link(g, chunk, 0).wait_recv()
        for d in (1, 2) if chunk >= cut else (1,):
            scan_out[g, chunk, d - 1] = (
                held(g, chunk, 0, d) + link_in[g, chunk, d].astype(F32)
            ).astype(BF16)
            if d == 1 and chunk % 2:
                pl.when(odd)(to_scan(g, chunk, 0).start)
                pl.when(even)(to_relay(g, chunk).start)
            else:
                to_scan(g, chunk, d - 1).start()
        if chunk >= cut:
            near[g, rows_of(chunk)] = held(g, chunk, 0, 0) + link_in[g, chunk, 0].astype(F32)

    def finish(g, chunk):
        if chunk < cut:
            to_link(g, chunk, 1).wait_recv()
            near[g, rows_of(chunk)] = (
                held(g, chunk, 0, 0)
                + zed_in[g, chunk, 0].astype(F32)
                + link_in[g, chunk, 0].astype(F32)
            )
        to_scan(g, chunk, 0).wait_recv()
        far[g, rows_of(chunk)] = scan_in[g, chunk, 0].astype(F32)
        if chunk >= cut:
            to_scan(g, chunk, 1).wait_recv()
            near[g, rows_of(chunk)] += scan_in[g, chunk, 1].astype(F32)

    low_rows = strip_rows // 4
    halves = [pl.ds(0, low_rows), pl.ds(low_rows, strip_rows - low_rows)]
    hop_at = {(0, 0): 0, (0, 1): 1, (1, 0): 2, (1, 1): 3, (2, 0): 4}
    step_at = {(1, 0, 0): 0, (1, 0, 1): 1, (2, 0, 0): 2, (2, 0, 1): 3, (2, 1, 1): 4}

    def over_link(d, g, h):
        at = hop_at[d, h]
        return remote(
            parts_ref.at[d, 0, g, halves[h]], parts_ref.at[d, 1, g, halves[h]],
            hop_send.at[g, at], hop_recv.at[g, at], link_mate,
        )

    def over_core(d, s, g, h):
        at = d * 2 + s
        return remote(
            parts_ref.at[d, s, g, halves[h]], parts_ref.at[d, s + 2, g, halves[h]],
            join_send.at[g, at, h], join_recv.at[g, at, h], core_mate,
        )

    def over_scan(d, s, g, h):
        at = step_at[d, s, h]
        source = own_far.at[g] if d == 1 else parts_ref.at[0, s, g]
        return remote(
            source.at[halves[h]], parts_ref.at[d, s, g, halves[h]],
            step_send.at[g, at], step_recv.at[g, at], after[d - 1],
        )

    def far_relay(h):
        return remote(
            own_far.at[0, halves[h]], hop_in.at[halves[h]],
            far_send.at[h], far_recv.at[h], before[0],
        )

    def far_pass(h):
        return remote(
            hop_in.at[halves[h]], parts_ref.at[1, 0, 0, halves[h]],
            last_send.at[h], step_recv.at[0, step_at[1, 0, h]], after[1],
        )

    def by_columns(high, low, table):
        return three_products(high, low, tables_ref[table], tables_ref[table + 1])

    def transform(g):
        rows = strip_rows * share
        for half in range(2):
            block = (near if half == 0 else far)[g]
            tall = jnp.concatenate(
                [block[:, :share].reshape(rows, window), block[:, share:].reshape(rows, window)], axis=1
            )
            high, low = split_two(tall)
            done = by_columns(high, low, 0)
            for c in range(2):
                waves[c, half * rows : (half + 1) * rows, :] = done[:, c * window : (c + 1) * window]

        for p in range(0, share, 2):
            columns = []
            for k in range(2):
                columns.append(
                    jnp.concatenate(
                        [waves[c, pl.ds(p + k, window, stride=share), :] for c in range(2)], axis=0
                    )
                )
            high, low = split_two(jnp.concatenate(columns, axis=1))
            wave = three_products(tables_ref[4], tables_ref[5], high, low)
            wave_re, wave_im = wave[:window], wave[window:]
            at = g * share + p
            values = jnp.concatenate([measured[at], measured[at + 1]], axis=1)
            modulus = jnp.sqrt(wave_re * wave_re + wave_im * wave_im + ETA)
            keep_share = 1.0 - values / modulus
            high, low = split_two(jnp.concatenate([wave_re * keep_share, wave_im * keep_share], axis=0))
            back = three_products(tables_ref[6], tables_ref[7], high, low)
            for k in range(2):
                for c in range(2):
                    backs[c, pl.ds(p + k, window, stride=share), :] = back[
                        c * window : (c + 1) * window, k * window : (k + 1) * window
                    ]

        live = live_ref[g * share : (g + 1) * share][None]
        for half in (1, 0):
            tall = jnp.concatenate(
                [backs[c, half * rows : (half + 1) * rows, :] for c in range(2)], axis=1
            )
            high, low = split_two(tall)
            done = by_columns(high, low, 2)
            pieces = [
                done[:, c * window : (c + 1) * window].reshape(strip_rows, share, window) * live
                for c in range(2)
            ]
            value = jnp.concatenate(pieces, axis=1).astype(BF16)
            if half:
                own_far[g] = value
                for h in range(2):
                    if g == 0:
                        pl.when(even)(over_scan(1, 0, g, h).start)
                        pl.when(odd)(far_relay(h).start)
                    else:
                        over_scan(1, 0, g, h).start()
            else:
                parts_ref[0, 0, g] = value
                for h in (1, 0):
                    over_link(0, g, h).start()
                for h in range(2):
                    over_scan(2, 0, g, h).start()
                    over_core(0, 0, g, h).start()

    def got_scan(d, s, g, h, link):
        over_scan(d, s, g, h).wait_recv()
        if link:
            over_link(d, g, h).start()
        over_core(d, s, g, h).start()

    def got_link(d, g, h, scan):
        over_link(d, g, h).wait_recv()
        if scan:
            over_scan(2, 1, g, h).start()
        over_core(d, 1, g, h).start()

    def pass_far(h):
        @pl.when(even)
        def _():
            far_relay(h).wait_recv()
            far_pass(h).start()

    def relay(g):
        got_scan(1, 0, g, 0, True)
        got_scan(1, 0, g, 1, True)
        got_link(0, g, 1, True)
        got_link(0, g, 0, False)
        got_scan(2, 0, g, 0, True)
        got_scan(2, 0, g, 1, False)
        got_link(1, g, 0, False)
        got_link(1, g, 1, False)
        got_scan(2, 1, g, 1, False)
        got_link(2, g, 0, False)

    early = range(cut)
    for chunk in range(chunks):
        compute(chunk)
        if chunk:
            after_core(0, chunk - 1)
            if chunk - 1 in early:
                after_core(1, chunk - 1)
    after_core(0, chunks - 1)
    for chunk in early:
        after_zed(0, chunk)
    for chunk in range(cut, chunks):
        after_core(1, chunk)
    for at in range(0, matrix_ref.shape[0], window):
        turned_ref[:, at : at + window] = matrix_ref[at : at + window, :].astype(F32).T.astype(BF16)
    for chunk in early:
        after_link(0, chunk)
        after_zed(1, chunk)
    for chunk in range(cut, chunks):
        after_link(0, chunk)
    for chunk in range(1, chunks, 2):
        pass_on(0, chunk)
    for chunk in early:
        after_link(1, chunk)
    for chunk in range(chunks):
        finish(0, chunk)
    side_loads[2].wait()
    side_loads[3].wait()
    transform(0)
    for chunk in range(cut, chunks):
        after_link(1, chunk)
    for chunk in range(1, chunks, 2):
        pass_on(1, chunk)
    for h in range(2):
        pass_far(h)
    for chunk in range(chunks):
        finish(1, chunk)
    transform(1)
    for g in range(groups):
        relay(g)

    for chunk in range(chunks):
        to_core(chunk).wait_send()
        for g in range(groups):
            to_link(g, chunk, 0).wait_send()
            if chunk % 2:
                pl.when(odd)(to_scan(g, chunk, 0).wait_send)
                pl.when(even)(to_relay(g, chunk).wait_send)
                pl.when(odd)(from_relay(g, chunk).wait_send)
            else:
                to_scan(g, chunk, 0).wait_send()
            if chunk < cut:
                to_link(g, chunk, 1).wait_send()
                to_zed(g, chunk).wait_send()
            else:
                to_scan(g, chunk, 1).wait_send()
    for g in range(groups):
        for d in range(3):
            for s in range(2):
                for h in range(2):
                    over_core(d, s, g, h).wait()
        for d, h in hop_at:
            over_link(d, g, h).wait_send()
        for d, s, h in step_at:
            if d == 1 and g == 0:
                pl.when(even)(over_scan(d, s, g, h).wait_send)
                pl.when(odd)(far_relay(h).wait_send)
                pl.when(even)(far_pass(h).wait_send)
            else:
                over_scan(d, s, g, h).wait_send()


def waves_to_gradients(per_tile, spots, freq, amp, live, tables, strip, amplitude, shares, scan_size,
                       groups=2, block_rows=8):
    _, beams, strip_rows, window = strip.shape
    share_rows = per_tile // shares
    group = 2 * share_rows
    depth = group // groups
    field_rows = strip_rows * scan_size
    chunks = strip_rows // block_rows
    cut = chunks // 2
    pairs = shares // 2
    assert groups == 2 and shares == 4 and scan_size > 4 and scan_size % 2 == 0 and chunks % 4 == 0
    assert field_rows & (field_rows - 1) == 0 and window & (window - 1) == 0
    tail = (block_rows, depth, window)
    vmem = pl.BlockSpec(memory_space=pltpu.VMEM)
    hbm = pl.BlockSpec(memory_space=pltpu.HBM)
    dma = pltpu.SemaphoreType.DMA
    stays = [
        pltpu.with_memory_space_constraint(v, pltpu.HBM) for v in (freq, amp, tables, strip, amplitude)
    ]
    return pl.pallas_call(
        functools.partial(wave_kernel, shares, scan_size),
        out_shape=[
            jax.ShapeDtypeStruct((3, shares, groups, strip_rows, depth, window), BF16),
            jax.ShapeDtypeStruct((2 * beams, 3 * shares * group), BF16),
            jax.ShapeDtypeStruct((2, shares * group, window), jnp.int32),
        ],
        in_specs=[vmem] * 2 + [hbm] * 5,
        out_specs=[vmem] * 3,
        scratch_shapes=[
            pltpu.VMEM((3 * shares * group, 2 * beams), BF16),
            pltpu.VMEM(freq.shape, jnp.int32),
            pltpu.VMEM(amp.shape, F32),
            pltpu.VMEM(tables.shape, BF16),
            pltpu.VMEM((2,) + spots.shape, jnp.int32),
            pltpu.VMEM((2, window, window), jnp.int32),
            pltpu.VMEM((2, 2, beams, block_rows, window), BF16),
            pltpu.VMEM((2 * beams * block_rows, window), F32),
            pltpu.VMEM((chunks, pairs, 3, block_rows, group, window), F32),
            pltpu.VMEM((chunks, pairs, 3, block_rows, group, window), BF16),
            pltpu.VMEM((chunks, pairs, 3, block_rows, group, window), BF16),
            pltpu.VMEM((groups, chunks, 3) + tail, BF16),
            pltpu.VMEM((groups, chunks, 3) + tail, BF16),
            pltpu.VMEM((groups, cut, 2) + tail, BF16),
            pltpu.VMEM((groups, cut, 2) + tail, BF16),
            pltpu.VMEM((groups, chunks, 2) + tail, BF16),
            pltpu.VMEM((groups, chunks, 2) + tail, BF16),
            pltpu.VMEM((groups, strip_rows, depth, window), F32),
            pltpu.VMEM((groups, strip_rows, depth, window), F32),
            pltpu.VMEM((share_rows, window, window), F32),
            pltpu.VMEM((2, window * share_rows // groups, window), F32),
            pltpu.VMEM((2, window * share_rows // groups, window), F32),
            pltpu.VMEM((groups, strip_rows, depth, window), BF16),
            dma((2,)),
            dma((4,)),
            dma((2,)),
            dma((2,)),
            dma((chunks,)),
            dma((chunks,)),
            dma((groups, chunks, 2)),
            dma((groups, chunks, 2)),
            dma((groups, cut)),
            dma((groups, cut)),
            dma((groups, chunks, 2)),
            dma((groups, chunks, 2)),
            dma((groups, 5)),
            dma((groups, 5)),
            dma((groups, 5)),
            dma((groups, 5)),
            dma((groups, 6, 2)),
            dma((groups, 6, 2)),
            pltpu.VMEM((groups, chunks // 2) + tail, BF16),
            pltpu.VMEM((strip_rows, depth, window), BF16),
            dma((groups, chunks // 2)),
            dma((groups, chunks // 2)),
            dma((groups, chunks // 2)),
            dma((2,)),
            dma((2,)),
            dma((2,)),
        ],
        compiler_params=pltpu.CompilerParams(
            collective_id=0, has_side_effects=True, vmem_limit_bytes=40 << 20
        ),
        cost_estimate=pl.CostEstimate(
            flops=12 * per_tile * beams * strip_rows * window,
            bytes_accessed=4 * beams * strip_rows * window,
            transcendentals=0,
        ),
    )(spots, live, *stays)


def backward_kernel(block_rows, offset_ref, matrix_ref, parts_ref, out_ref, wide):
    depth = matrix_ref.shape[0]
    window = out_ref.shape[3]
    first = pl.program_id(0) * block_rows
    kinds, shares, groups = parts_ref.shape[:3]
    for row in range(0, block_rows, 2):
        sides = []
        for k in range(2):
            here = first + row + k
            strips = []
            for d in range(kinds):
                tall = jnp.concatenate(
                    [parts_ref[d, s, g, row + k] for s in range(shares) for g in range(groups)], axis=0
                )
                if d == 0:
                    tall = jnp.where(here >= offset_ref[0], tall.astype(F32), 0.0).astype(BF16)
                if d == 2:
                    tall = jnp.where(here < offset_ref[1], tall.astype(F32), 0.0).astype(BF16)
                strips.append(tall)
            sides.append(jnp.concatenate(strips, axis=0))
        sums = jnp.dot(
            matrix_ref[...], jnp.concatenate(sides, axis=1), preferred_element_type=F32
        )
        for k in range(2):
            wide[pl.ds(row + k, depth, stride=block_rows), :] = sums[:, k * window : (k + 1) * window]
    out_ref[...] = wide[...].reshape(out_ref.shape).astype(BF16)


def backward(matrix, offsets, parts, beams, block_rows=8):
    kinds, shares, groups, strip_rows, depth, window = parts.shape
    return pl.pallas_call(
        functools.partial(backward_kernel, block_rows),
        grid=(strip_rows // block_rows,),
        out_shape=jax.ShapeDtypeStruct((2, beams, strip_rows, window), BF16),
        in_specs=[
            pl.BlockSpec(offsets.shape, lambda i: (0, 0, 0)),
            pl.BlockSpec(matrix.shape, lambda i: (0, 0)),
            pl.BlockSpec(
                (kinds, shares, groups, block_rows, depth, window), lambda i: (0, 0, 0, i, 0, 0)
            ),
        ],
        out_specs=pl.BlockSpec((2, beams, block_rows, window), lambda i: (0, 0, i, 0)),
        scratch_shapes=[pltpu.VMEM((2 * beams * block_rows, window), F32)],
        compiler_params=pltpu.CompilerParams(vmem_limit_bytes=28 << 20),
        cost_estimate=pl.CostEstimate(
            flops=2 * matrix.size * strip_rows * window,
            bytes_accessed=4 * beams * strip_rows * window + 2 * parts.size,
            transcendentals=0,
        ),
    )(offsets, matrix, parts)


def transform_tables(window):
    counter = np.arange(window)
    turn_angle = (counter[:, None] * counter[None, :] % window) * (2.0 * np.pi / window)
    table_re = np.cos(turn_angle) / np.sqrt(window)
    table_im = -np.sin(turn_angle) / np.sqrt(window)
    stacked = []
    for left in (False, True):
        for sign in (1.0, -1.0):
            imag = sign * table_im
            if left:
                full = np.block([[table_re, -imag], [imag, table_re]])
            else:
                full = np.block([[table_re, imag], [-imag, table_re]])
            high = full.astype(BF16)
            stacked += [high, (full - high.astype(np.float64)).astype(BF16)]
    return jnp.asarray(np.stack(stacked))


def body(smatrix, beam_freq, beam_amp, row_offset, col_offset, counts, amplitude):
    beam_dev = smatrix.shape[1]
    window = smatrix.shape[3]
    per_tile = row_offset.shape[0]
    scan_size = lax.axis_size("scan")
    shares = lax.axis_size("beam")
    share_rows = per_tile // shares
    assert window == 2 * smatrix.shape[2]
    assert per_tile <= window
    spots = jnp.pad(jnp.stack([row_offset, col_offset]), ((0, 6), (0, window - per_tile)))
    first_row = lax.axis_index("beam") * share_rows
    live = (first_row + jnp.arange(share_rows, dtype=jnp.int32) < counts[0]).astype(F32)
    live = jnp.broadcast_to(live[:, None], (share_rows, window))
    parts, matrix, offsets = waves_to_gradients(
        per_tile, spots, beam_freq, beam_amp, live, transform_tables(window), smatrix, amplitude, shares, scan_size
    )
    return backward(matrix, offsets, parts, beam_dev)


def solution(mesh):
    return jax.shard_map(
        body,
        mesh=mesh,
        in_specs=(
            P(None, "beam", "scan", None),
            P(None, "beam"),
            P(None, "beam"),
            P("scan"),
            P("scan"),
            P("scan"),
            P("scan", None, None),
        ),
        out_specs=P(None, "beam", "scan", None),
        check_vma=False,
    )
```
